32 devices in a mesh: grp: 2 (over y), ka: 16 (over z, x, core).
Axes of the slice: x: 2, y: 2, z: 4, core: 2. Of those that a mesh axis runs over, the one named last changes fastest.
Arguments:
- eigvecs: bfloat16 [16, 2, 64, 1024], P('ka'), may hold values from -0.25 to 0.25
- eigvals: bfloat16 [496, 2, 512], P('ka'), may hold values from -2 to 2
- kpoints: bfloat16 [3, 496], P(None, 'ka'), may hold values from 0 to 1
- counts: int32 [16], P('ka'), may hold values from 1 to 31, as said below
- energy_real: float32 [2], P('grp'), parts along dimension 0, may hold values from -0.5 to 0.5
- energy_imag: float32 [2], P('grp'), parts along dimension 0, may hold values from 0.1 to 0.4
- offsets: int32 [3, 16], replicated, may hold values from -4 to 4, as said below
- atom_orbitals: int32 [8], replicated, may hold values from 1 to 12, 64 in all
- positions: float32 [3, 8], replicated, may hold values from 0 to 1
- exch_split: float32 [64, 64], replicated, may hold values from -6 to 6
Outputs:
- exchange: float32 [32, 8, 8], P(('grp', 'ka')), parts along dimension 0
The draws below stay inside these ranges and needn't reach their ends.
There are 2 independent parts, one for each index of `grp`. The reference program is written for one: setup_inputs(seed, part) draws one part's arguments, and reference() takes and returns one part's arrays. A program takes and returns all parts, laid end to end along the dimension named above; an argument that names none is the same for every part. Nothing has to cross between parts.
Inputs may be any that keep to these rules, and one draw needn't show every extreme that they name: For every device d below the axis's middle, counts[d] + counts[d + 8] is at most 32, one of the two exceeds 16, and the pair of device 0 reaches the maximum count. `offsets`: for r < 8, column r + 8 is minus column r, and the first component of column r is 1 to 4.
All inputs are finite; a program needn't handle non-finite values.
Results may differ from the reference program's by a relative error of at most 0.0063.
The reference program's roundings to bfloat16 on the way count: a program that leaves them out, or rounds other values in their place, can miss the bound.
Values may be sent and summed in bfloat16 or wider, within the bound.
No kernel may reach another device: no remote copies, remote signals or barrier semaphores. Data moves between devices by JAX's collectives and lax.ppermute only.
A program may use at most 128 MiB of HBM per device.

```python
import math
import jax
import jax.numpy as jnp
import numpy as np
from jax import lax

NORB = 512
MO = 64
NA = 8
MOST = 12
R_DEV = 1
KB = 16
KTOT = 496
N_KA = 16


def draw_counts(key, part):
    half_axis = N_KA // 2
    first_key, second_key, third_key = jax.random.split(jax.random.fold_in(key, 11), 3)
    busy_count = jax.random.randint(first_key, (half_axis,), KB + 1, 2 * KB)
    busy_count = busy_count.at[0].set(2 * KB - 1)
    spare_room = 2 * KB - busy_count
    drawn_count = 1 + jax.random.randint(second_key, (half_axis,), 0, 1 << 20) % spare_room
    which_first = jax.random.randint(third_key, (half_axis,), 0, 2)
    first_half = jnp.where(which_first == 1, busy_count, drawn_count)
    second = jnp.where(which_first == 1, drawn_count, busy_count)
    return jnp.concatenate([first_half, second]).astype(jnp.int32)


def draw_offsets(key, part):
    half_rows = R_DEV * N_KA // 2
    first_key, second_key = jax.random.split(jax.random.fold_in(key, 23), 2)
    leading = jax.random.randint(first_key, (1, half_rows), 1, 5)
    others = jax.random.randint(second_key, (2, half_rows), -4, 5)
    front = jnp.concatenate([leading, others], 0)
    return jnp.concatenate([front, -front], 1).astype(jnp.int32)


def block_scale(own_key, extent, cuts, smallest, high):
    gain, own = 1.0, jax.random.fold_in(own_key, 6)
    for axis_at, shards_of in cuts:
        steps = jnp.exp(jax.random.uniform(jax.random.fold_in(own, axis_at), (shards_of,), jnp.float32, smallest / len(cuts), high / len(cuts)))
        gain = gain * jnp.repeat(steps, extent[axis_at] // shards_of).reshape([-1 if axis == axis_at else 1 for axis in range(len(extent))])
    return gain


def profile(number_of, total, most, lean):
    portions = [(1 << 20) // math.isqrt(rank ** lean) + 1 for rank in range(2, number_of + 1)]
    rest, given = total - most - (number_of - 1), [1] * (number_of - 1)
    while rest > 0:
        candidates = [i for i in range(number_of - 1) if given[i] < most]
        pool, left = sum([portions[i] for i in candidates]), rest
        for i in candidates:
            extra = min(most - given[i], max(1, left * portions[i] // pool), rest)
            given[i] = given[i] + extra
            rest = rest - extra
    return np.array([most] + given)


def uneven(rng, count, total, limit, slope):
    if count == 2:
        one = jax.random.randint(rng, (), max(1, total - limit), min(limit, total - 1) + 1)
        return jnp.stack([one, total - one])
    lengths = jnp.asarray(profile(count, total, limit, slope), jnp.int32)
    twos = (count - 1) // 2
    donor, receiver = lengths[1:1 + 2 * twos:2], lengths[2:2 + 2 * twos:2]
    room = jnp.minimum(donor - 1, limit - receiver)
    moved = jax.random.randint(jax.random.fold_in(rng, 1), (twos,), 0, 1 << 20) % (room + 1)
    lengths = lengths.at[1:1 + 2 * twos:2].set(donor - moved).at[2:2 + 2 * twos:2].set(receiver + moved)
    return lengths[jax.random.permutation(jax.random.fold_in(rng, 2), count)]


def bell_draw(stream_key, extent, deviation, limit, cuts=(), kind=jnp.bfloat16):
    result = jax.random.normal(stream_key, extent, jnp.float32) * deviation
    if len(cuts) > 0:
        result = block_scale(stream_key, extent, cuts, -0.22, 0.18) * result
    return jnp.clip(result, min=-limit, max=limit).astype(kind)


def setup_inputs(seed: int = 0, part: int = 0) -> dict:
    splits = jax.random.split(jax.random.key(seed), 11)
    own_keys = jax.random.split(jax.random.fold_in(splits[10], part), 11)
    eigvecs = bell_draw(splits[0], (N_KA, 2, MO, 2 * NORB), NORB ** -0.5, 0.25, ((0, 16),))
    eigvals = jnp.clip(jax.random.uniform(splits[1], (KTOT, 2, NORB), jnp.float32, -2.0, 2.0) * block_scale(splits[1], (KTOT, 2, NORB), ((0, 16),), -0.4, 0.0), -2.0, 2.0).astype(jnp.bfloat16)
    kpoints = jnp.clip(1.0 * jax.random.uniform(splits[2], (3, KTOT), jnp.float32) ** block_scale(splits[2], (3, KTOT), ((1, 16),), -0.2, 0.2), 0.0, 1.0).astype(jnp.bfloat16)
    counts = draw_counts(jax.random.fold_in(splits[10], 71), part)
    energy_real = jnp.clip(jax.random.uniform(own_keys[4], (1,), jnp.float32, -0.5, 0.5), -0.5, 0.5)
    energy_imag = jnp.clip(jax.random.uniform(own_keys[5], (1,), jnp.float32, 0.1, 0.4), 0.1, 0.4)
    offsets = draw_offsets(jax.random.fold_in(splits[10], 71), part)
    atom_orbitals = uneven(splits[7], NA, MO, MOST, 0).astype(jnp.int32)
    positions = jnp.clip(jax.random.uniform(splits[8], (3, NA), jnp.float32, 0.0, 1.0), 0.0, 1.0)
    exch_split = bell_draw(splits[9], (MO, MO), 1.0, 6.0, (), jnp.float32)
    return {"eigvecs": eigvecs, "eigvals": eigvals, "kpoints": kpoints, "counts": counts, "energy_real": energy_real, "energy_imag": energy_imag, "offsets": offsets, "atom_orbitals": atom_orbitals, "positions": positions, "exch_split": exch_split}


inv_four_pi = 0.25 / 3.141592653589793
two_pi = 2.0 * 3.141592653589793


def member_table(atom_orbitals, mag):
    ends = jnp.cumsum(atom_orbitals)
    starts = ends - atom_orbitals
    orbital = jnp.arange(mag, dtype=jnp.int32)[:, None]
    return ((orbital >= starts[None, :]) & (orbital < ends[None, :])).astype(jnp.float32)


def bare_green(vectors, levels, energy_real, energy_imag):
    norb = levels.shape[-1]
    levels_wide = levels.astype(jnp.float32)
    shift = energy_real[0] - levels_wide
    denom = shift * shift + energy_imag[0] * energy_imag[0]
    real_factor = (shift / denom)[:, :, None, :]
    imag_factor = (-energy_imag[0] / denom)[:, :, None, :]
    wide = vectors.astype(jnp.float32)
    re_vec = wide[..., :norb]
    im_vec = wide[..., norb:]
    scaled = jnp.concatenate([re_vec * real_factor - im_vec * imag_factor,
                              re_vec * imag_factor + im_vec * real_factor], -1).astype(jnp.bfloat16)
    right = jnp.concatenate([vectors, jnp.concatenate([-vectors[..., norb:], vectors[..., :norb]], -1)], axis=-2)
    return jnp.einsum('ksan,scn->ksac', scaled.astype(jnp.float32), right.astype(jnp.float32),
                      precision=lax.Precision.HIGHEST)


def apply_gauge(product, coords, site):
    mag = site.shape[1]
    kpos = jnp.einsum('xk,xa->ka', coords.astype(jnp.float32), site, precision=lax.Precision.HIGHEST)
    phase = two_pi * (kpos[:, None, :] - kpos[:, :, None])
    cos_phase = jnp.cos(phase)[:, None]
    sin_phase = jnp.sin(phase)[:, None]
    green_re = product[..., :mag]
    green_im = product[..., mag:]
    new_re = green_re * cos_phase - green_im * sin_phase
    new_im = green_re * sin_phase + green_im * cos_phase
    stacked = jnp.stack([new_re, new_im], axis=2)
    return stacked.reshape(product.shape[0], 2, 2, mag * mag).astype(jnp.bfloat16)


def phase_terms(coords, slot_weights, lattice, grid, blocks):
    angle = two_pi * jnp.einsum('ck,cr->rk', coords.astype(jnp.float32), lattice.astype(jnp.float32),
                                precision=lax.Precision.HIGHEST)
    weight_wide = slot_weights.astype(jnp.float32)[None, :]
    cos_weight = (jnp.cos(angle) * weight_wide).astype(jnp.bfloat16)
    sin_weight = (jnp.sin(angle) * weight_wide).astype(jnp.bfloat16)

    def matmul(left, right):
        return jnp.dot(left, right, preferred_element_type=jnp.float32)

    def combine(sign, spin):
        real_sum = matmul(cos_weight, grid[:, spin, 0]) + sign * matmul(sin_weight, grid[:, spin, 1])
        imag_sum = matmul(cos_weight, grid[:, spin, 1]) - sign * matmul(sin_weight, grid[:, spin, 0])
        return [real_sum, imag_sum]

    pieces = combine(1.0, 0) + combine(1.0, 1)
    if blocks == 3:
        pieces = pieces + combine(-1.0, 1)
    return jnp.concatenate(pieces, axis=1)


def pair_exchange(up_block, down_block, exch_split, atom_orbitals):
    mag = exch_split.shape[0]
    rows = up_block.shape[0]
    area = mag * mag
    up_re = up_block[:, :area].reshape(rows, mag, mag)
    up_im = up_block[:, area:].reshape(rows, mag, mag)
    down_re = down_block[:, :area].reshape(rows, mag, mag)
    down_im = down_block[:, area:].reshape(rows, mag, mag)
    member = member_table(atom_orbitals, mag)
    same_atom = jnp.dot(member, member.T, precision=lax.Precision.HIGHEST)
    splitting = 0.5 * (exch_split + exch_split.T) * same_atom
    high = lax.Precision.HIGHEST
    left_re = jnp.einsum('ab,rbc->rac', splitting, up_re, precision=high)
    left_im = jnp.einsum('ab,rbc->rac', splitting, up_im, precision=high)
    right_re = jnp.einsum('ab,rbc->rac', splitting, down_re, precision=high)
    right_im = jnp.einsum('ab,rbc->rac', splitting, down_im, precision=high)
    im_part = left_re * jnp.swapaxes(right_im, 1, 2) + left_im * jnp.swapaxes(right_re, 1, 2)
    return -inv_four_pi * jnp.einsum('ai,rab,bj->rij', member, im_part, member, precision=high)


def reference(eigvecs, eigvals, kpoints, counts, energy_real, energy_imag, offsets, atom_orbitals, positions,
              exch_split):
    batches = counts.shape[0]
    kslot = eigvals.shape[0] // batches
    mag = eigvecs.shape[2]
    norb = eigvals.shape[2]
    area = mag * mag
    slot_index = jnp.arange(kslot, dtype=jnp.int32)
    inverse = (1.0 / counts.astype(jnp.float32)).astype(jnp.bfloat16)
    weights = jnp.where(slot_index[None, :] < counts[:, None], inverse[:, None],
                        jnp.zeros((), jnp.bfloat16))
    member = member_table(atom_orbitals, mag)
    site = jnp.dot(positions, member.T, precision=lax.Precision.HIGHEST)
    level_blocks = eigvals.reshape(batches, kslot, 2, norb)
    coord_blocks = jnp.transpose(kpoints.reshape(3, batches, kslot), (1, 0, 2))

    def step(total, batch):
        vectors, levels, coords, slot_weights = batch
        grid = apply_gauge(bare_green(vectors, levels, energy_real, energy_imag), coords, site)
        return total + phase_terms(coords, slot_weights, offsets, grid, 3), None

    start = jnp.zeros((offsets.shape[1], 6 * area), jnp.float32)
    terms, unused = lax.scan(step, start, (eigvecs, level_blocks, coord_blocks, weights))
    return pair_exchange(terms[:, :2 * area], terms[:, 4 * area:], exch_split, atom_orbitals)
```

```python
import functools

import jax
import jax.numpy as jnp
from jax import lax
from jax.experimental import pallas as pl
from jax.experimental.pallas import tpu as pltpu
from jax.sharding import PartitionSpec as P


inv_four_pi = 0.25 / 3.141592653589793
two_pi = 2.0 * 3.141592653589793
f32 = jnp.float32
bf16 = jnp.bfloat16
LANES = 128
SUB = 8


def iota(shape, dim):
    return lax.broadcasted_iota(jnp.int32, shape, dim)


def column_of(row, count):
    diag = iota((count, count), 0) == iota((count, count), 1)
    return jnp.sum(jnp.where(diag, row, jnp.zeros_like(row)), axis=1, keepdims=True)


def spans_down(orb_row, count):
    before = iota((count, count), 1) < iota((count, count), 0)
    starts = jnp.sum(jnp.where(before, orb_row, 0.0), axis=1, keepdims=True)
    return starts, starts + column_of(orb_row, count)


def spans_across(orb_row, count):
    before = iota((count, count), 0) < iota((count, count), 1)
    starts = jnp.sum(jnp.where(before, column_of(orb_row, count), 0.0), axis=0, keepdims=True)
    return starts, starts + orb_row


def green_kernel(
    axis,
    nslot,
    r_dev,
    vec_ref,
    lev_ref,
    k_ref,
    cnt_ref,
    er_ref,
    ei_ref,
    off_ref,
    orb_ref,
    pos_ref,
    keep_ref,
    send_ref,
    kpad_ref,
    right_ref,
    sum_ref,
    f1_ref,
    f2_ref,
    f3_ref,
    *scaled_refs,
):
    mag, norb = vec_ref.shape[2], vec_ref.shape[3] // 2
    natom = orb_ref.shape[1]
    srow = lev_ref.shape[1]
    total = off_ref.shape[1]
    half = total // 2
    group = 256 // srow
    me = lax.axis_index(axis)

    er, ei = er_ref[...], ei_ref[...]
    for spin in range(2):
        shift = er - lev_ref[spin]
        inv = 1.0 / (shift * shift + ei * ei)
        fr = shift * inv
        fi = -(ei * inv)
        f1_ref[spin] = fr
        f2_ref[spin] = fi - fr
        f3_ref[spin] = fi + fr
        re_vec = vec_ref[0, spin, :, :norb]
        im_vec = vec_ref[0, spin, :, norb:]
        right_ref[spin, :mag, :norb] = re_vec
        right_ref[spin, :mag, norb:] = im_vec
        right_ref[spin, mag:, :norb] = -im_vec
        right_ref[spin, mag:, norb:] = re_vec
        re_wide = re_vec.astype(f32)
        im_wide = im_vec.astype(f32)
        sum_ref[spin, 0] = re_wide + im_wide
        sum_ref[spin, 1] = re_wide
        sum_ref[spin, 2] = im_wide

    kpad_ref[...] = jnp.zeros_like(kpad_ref)
    kpad_ref[0:3, 0:nslot] = k_ref[...].astype(f32)
    kwide = kpad_ref[...]
    ktall = kwide.T
    klane = kwide
    for step in range(1, LANES // srow):
        klane = klane + pltpu.roll(kwide, step * srow, 1)
    klane = jnp.concatenate([klane] * (group * srow // LANES), axis=1)

    orb_row = orb_ref[...].astype(f32)
    starts, ends = spans_down(orb_row, natom)
    lane = iota((natom, LANES), 1)
    orbital = jnp.where(lane >= mag, lane - mag, lane).astype(f32)
    inside = (orbital >= starts) & (orbital < ends)
    kpos = jnp.zeros((srow, LANES), f32)
    for x in range(3):
        pos_col = column_of(pos_ref[x : x + 1, :], natom)
        site = jnp.sum(jnp.where(inside, pos_col, 0.0), axis=0, keepdims=True)
        kpos = kpos + ktall[0:srow, x : x + 1] * site
    cos_pos = jnp.cos(two_pi * kpos)
    sin_pos = jnp.sin(two_pi * kpos)
    first = iota((srow, LANES), 1) < mag
    cos_sgn = jnp.where(first, -cos_pos, cos_pos)
    sin_sgn = jnp.where(first, -sin_pos, sin_pos)

    slot = iota((1, group * srow), 1) % srow
    count = cnt_ref[...]
    inverse = (1.0 / count.astype(f32)).astype(bf16).astype(f32)
    weight = jnp.where(slot < count, inverse, 0.0)
    own = (iota((SUB, group * srow), 1) // srow) == iota((SUB, group * srow), 0)
    blocks = []
    for base in range(0, half, SUB):
        place = iota((SUB, total), 0) + base
        owner = place // r_dev if r_dev > 1 else place
        wanted = owner ^ me
        if r_dev > 1:
            wanted = wanted * r_dev + place % r_dev
        pick = iota((SUB, total), 1) == wanted
        angle = jnp.zeros((SUB, group * srow), f32)
        for x in range(3):
            off = jnp.where(pick, off_ref[x : x + 1, :].astype(f32), 0.0)
            angle = angle + jnp.sum(off, axis=1, keepdims=True) * klane[x : x + 1, :]
        angle = two_pi * angle
        rows = []
        for wave in (jnp.cos(angle) * weight, jnp.sin(angle) * weight):
            for r in range(SUB):
                rows.append(jnp.where(own, wave[r : r + 1, :], 0.0))
        blocks.append(jnp.concatenate(rows, axis=0).astype(bf16))

    flip = jnp.where(iota((SUB, LANES), 1) < mag, 1.0, -1.0).astype(f32)
    for c in range(mag // group):
        green = []
        for spin in range(2):
            buf = scaled_refs[(c % 2) * 2 + spin]
            for j in range(group):
                a = c * group + j
                both = f1_ref[spin] * sum_ref[spin, 0, a : a + 1, :]
                cross = f2_ref[spin] * sum_ref[spin, 1, a : a + 1, :]
                other = f3_ref[spin] * sum_ref[spin, 2, a : a + 1, :]
                buf[j * srow : (j + 1) * srow, :norb] = (both - other).astype(bf16)
                buf[j * srow : (j + 1) * srow, norb:] = (both + cross).astype(bf16)
            green.append(
                lax.dot_general(
                    buf[...],
                    right_ref[spin],
                    (((1,), (1,)), ((), ())),
                    preferred_element_type=f32,
                )
            )
        turned = [[], []]
        for j in range(group):
            a = c * group + j
            cos_a, sin_a = cos_pos[:, a : a + 1], sin_pos[:, a : a + 1]
            cos_phase = cos_pos * cos_a + sin_pos * sin_a
            sin_phase = sin_sgn * cos_a - cos_sgn * sin_a
            for spin in range(2):
                g = green[spin][j * srow : (j + 1) * srow, :]
                turned[spin].append(g * cos_phase + pltpu.roll(g, mag, 1) * sin_phase)
        stack = jnp.concatenate(
            [jnp.concatenate(turned[spin], axis=0).astype(bf16) for spin in range(2)], axis=1
        )
        for b, block in enumerate(blocks):
            res = jnp.dot(block, stack, preferred_element_type=f32)
            for r in range(SUB):
                plus, minus = [], []
                for spin in range(2):
                    lanes = slice(spin * LANES, (spin + 1) * LANES)
                    even = res[r * SUB : (r + 1) * SUB, lanes]
                    odd = res[(SUB + r) * SUB : (SUB + r + 1) * SUB, lanes]
                    odd = pltpu.roll(odd, mag, 1) * flip
                    plus.append(even + odd if spin == 0 else even - odd)
                    minus.append(even - odd if spin == 0 else even + odd)
                for p, pieces in ((b * SUB + r, plus), (b * SUB + r + half, minus)):
                    owner, inner = p // r_dev, p % r_dev
                    row = (owner // 2) * r_dev + inner
                    block_out = jnp.concatenate(pieces, axis=0)
                    rows = slice(c * 2 * group, (c + 1) * 2 * group)
                    if owner % 2 == 0:
                        keep_ref[row, rows, :] = block_out
                    else:
                        send_ref[row, rows, :] = block_out.astype(bf16)


def add_kernel(r_dev, keep_ref, got_ref, next_ref, send_ref):
    for q in range(keep_ref.shape[0]):
        owner, inner = q // r_dev, q % r_dev
        row = (owner // 2) * r_dev + inner
        value = keep_ref[q] + got_ref[q].astype(f32)
        if owner % 2 == 0:
            next_ref[row] = value
        else:
            send_ref[row] = value.astype(bf16)


def exchange_kernel(group, keep_ref, got_ref, orb_ref, split_ref, out_ref):
    mag = split_ref.shape[0]
    natom = orb_ref.shape[1]
    high = lax.Precision.HIGHEST
    orb_row = orb_ref[...].astype(f32)
    starts, ends = spans_across(orb_row, natom)
    orbital = iota((mag, natom), 0).astype(f32)
    member = jnp.where((orbital >= starts) & (orbital < ends), 1.0, 0.0)
    starts, ends = spans_down(orb_row, natom)
    orbital = iota((natom, mag), 1).astype(f32)
    member_t = jnp.where((orbital >= starts) & (orbital < ends), 1.0, 0.0)
    same_atom = jnp.dot(member, member_t, preferred_element_type=f32)
    split = split_ref[...]
    splitting = 0.5 * (split + split.T) * same_atom
    for row in range(keep_ref.shape[0]):
        value = keep_ref[row] + got_ref[row].astype(f32)
        up, down = [], []
        for c in range(mag // group):
            up.append(value[c * 2 * group : c * 2 * group + group])
            down.append(value[c * 2 * group + group : (c + 1) * 2 * group])
        up = jnp.concatenate(up, axis=0)
        down = jnp.concatenate(down, axis=0)
        both = jnp.concatenate([up, down], axis=1)
        both = jnp.dot(splitting, both, precision=high, preferred_element_type=f32)
        left = both[:, :LANES]
        right = both[:, LANES:].T
        im_part = left[:, :mag] * right[mag:, :] + left[:, mag:] * right[:mag, :]
        part = jnp.dot(member_t, im_part, precision=high, preferred_element_type=f32)
        part = jnp.dot(part, member, precision=high, preferred_element_type=f32)
        out_ref[row] = -inv_four_pi * part


def vmem(count):
    return [pl.BlockSpec(memory_space=pltpu.VMEM)] * count


def local(
    axis,
    n,
    eigvecs,
    eigvals,
    kpoints,
    counts,
    energy_real,
    energy_imag,
    offsets,
    atom_orbitals,
    positions,
    exch_split,
):
    nslot, _, norb = eigvals.shape
    mag = eigvecs.shape[2]
    total = offsets.shape[1]
    r_dev = total // n
    srow = -(-nslot // 32) * 32
    group = 256 // srow
    levels = jnp.pad(
        jnp.swapaxes(eigvals, 0, 1).astype(f32), ((0, 0), (0, srow - nslot), (0, 0))
    )
    orb = atom_orbitals[None, :]
    rows = total // 2
    keep, send = pl.pallas_call(
        functools.partial(green_kernel, axis, nslot, r_dev),
        out_shape=(
            jax.ShapeDtypeStruct((rows, 2 * mag, LANES), f32),
            jax.ShapeDtypeStruct((rows, 2 * mag, LANES), bf16),
        ),
        in_specs=vmem(9),
        out_specs=tuple(vmem(2)),
        scratch_shapes=[
            pltpu.VMEM((SUB, LANES), f32),
            pltpu.VMEM((2, 2 * mag, 2 * norb), bf16),
            pltpu.VMEM((2, 3, mag, norb), f32),
            pltpu.VMEM((2, srow, norb), f32),
            pltpu.VMEM((2, srow, norb), f32),
            pltpu.VMEM((2, srow, norb), f32),
        ]
        + [pltpu.VMEM((group * srow, 2 * norb), bf16)] * 4,
        compiler_params=pltpu.CompilerParams(vmem_limit_bytes=16 << 20),
        name="green",
    )(
        eigvecs,
        levels,
        kpoints,
        counts[None, :],
        energy_real[None, :],
        energy_imag[None, :],
        offsets,
        orb,
        positions,
    )
    bit = 1
    while True:
        got = lax.ppermute(send, axis, [(d, d ^ bit) for d in range(n)])
        bit *= 2
        if bit == n:
            break
        rows //= 2
        keep, send = pl.pallas_call(
            functools.partial(add_kernel, r_dev),
            out_shape=(
                jax.ShapeDtypeStruct((rows, 2 * mag, LANES), f32),
                jax.ShapeDtypeStruct((rows, 2 * mag, LANES), bf16),
            ),
            in_specs=vmem(2),
            out_specs=tuple(vmem(2)),
            compiler_params=pltpu.CompilerParams(vmem_limit_bytes=4 << 20),
            name="add",
        )(keep, got)
    natom = atom_orbitals.shape[0]
    return pl.pallas_call(
        functools.partial(exchange_kernel, group),
        out_shape=jax.ShapeDtypeStruct((r_dev, natom, natom), f32),
        in_specs=vmem(4),
        out_specs=vmem(1)[0],
        compiler_params=pltpu.CompilerParams(vmem_limit_bytes=4 << 20),
        name="exchange",
    )(keep, got, orb, exch_split)


def solution(mesh):
    placed = (
        P("ka", None, None, None),
        P("ka", None, None),
        P(None, "ka"),
        P("ka"),
        P("grp"),
        P("grp"),
        P(),
        P(),
        P(),
        P(),
    )
    return jax.shard_map(
        functools.partial(local, "ka", mesh.shape["ka"]),
        mesh=mesh,
        in_specs=placed,
        out_specs=P(("grp", "ka"), None, None),
        check_vma=False,
    )
```

```python
import functools

import jax
import jax.numpy as jnp
from jax import lax
from jax.experimental import pallas as pl
from jax.experimental.pallas import tpu as pltpu
from jax.sharding import PartitionSpec as P


inv_four_pi = 0.25 / 3.141592653589793
two_pi = 2.0 * 3.141592653589793
f32 = jnp.float32
bf16 = jnp.bfloat16
LANES = 128
SUB = 8
GROUPS = 4


def iota(shape, dim):
    return lax.broadcasted_iota(jnp.int32, shape, dim)


def spans(orb_ref):
    start, found = jnp.int32(0), []
    for i in range(orb_ref.shape[0]):
        stop = start + orb_ref[i]
        found.append((start, stop))
        start = stop
    return found


def split_two(x):
    high = x.astype(bf16)
    return high, (x - high.astype(f32)).astype(bf16)


def green_kernel(
    axis,
    r_dev,
    cnt_ref,
    er_ref,
    ei_ref,
    vec_hbm,
    lev_hbm,
    k_hbm,
    off_hbm,
    orb_hbm,
    pos_hbm,
    keep_ref,
    send_ref,
    vec_ref,
    lev_ref,
    k_ref,
    off_ref,
    orb_ref,
    pos_ref,
    sems,
    kpad_ref,
    wide_ref,
    cos_ref,
    sin_ref,
    right_ref,
    sum_ref,
    f1_ref,
    f2_ref,
    f3_ref,
    *scaled_refs,
):
    sources = (vec_hbm, lev_hbm, k_hbm, off_hbm, orb_hbm, pos_hbm)
    targets = (vec_ref, lev_ref, k_ref, off_ref, orb_ref, pos_ref)
    copies = [
        pltpu.make_async_copy(source, target, sems.at[i])
        for i, (source, target) in enumerate(zip(sources, targets))
    ]
    for copy in copies[::-1]:
        copy.start()

    nslot = lev_ref.shape[0]
    mag, norb = vec_ref.shape[2], vec_ref.shape[3] // 2
    natom = orb_ref.shape[0]
    srow = f1_ref.shape[1]
    total = off_ref.shape[1]
    half = total // 2
    group = 256 // srow
    me = lax.axis_index(axis)
    kpad_ref[...] = jnp.zeros_like(kpad_ref)
    wide_ref[...] = jnp.zeros_like(wide_ref)
    for i in (2, 3, 4, 5):
        copies[i].wait()

    kpad_ref[0:3, 0:nslot] = k_ref[...].astype(f32)
    kwide = kpad_ref[...]
    ktall = kwide.T
    klane = kwide
    for step in range(1, LANES // srow):
        klane = klane + pltpu.roll(kwide, step * srow, 1)

    bounds = spans(orb_ref)
    lane = iota((1, LANES), 1)
    orbital = jnp.where(lane >= mag, lane - mag, lane)
    kpos = jnp.zeros((srow, LANES), f32)
    kat = jnp.zeros((srow, LANES), f32)
    for x in range(3):
        site = jnp.zeros((1, LANES), f32)
        atom = jnp.zeros((1, LANES), f32)
        for i, (start, stop) in enumerate(bounds):
            where = pos_ref[x, i]
            site = jnp.where((orbital >= start) & (orbital < stop), where, site)
            atom = jnp.where(lane == i, where, atom)
        kpos = kpos + ktall[0:srow, x : x + 1] * site
        kat = kat + ktall[0:srow, x : x + 1] * atom
    cos_pos, sin_pos = jnp.cos(two_pi * kpos), jnp.sin(two_pi * kpos)
    cos_atom, sin_atom = jnp.cos(two_pi * kat), jnp.sin(two_pi * kat)
    first = iota((srow, LANES), 1) < mag
    cos_sgn = jnp.where(first, -cos_pos, cos_pos)
    sin_sgn = jnp.where(first, -sin_pos, sin_pos)
    for i in range(natom):
        cos_a, sin_a = cos_atom[:, i : i + 1], sin_atom[:, i : i + 1]
        cos_ref[i] = cos_pos * cos_a + sin_pos * sin_a
        sin_ref[i] = sin_sgn * cos_a - cos_sgn * sin_a

    lane = iota((1, LANES), 1) % srow
    count = cnt_ref[0]
    inverse = jnp.full((1, LANES), count, jnp.int32).astype(f32)
    inverse = (1.0 / inverse).astype(bf16).astype(f32)
    weight = jnp.where(lane < count, inverse, 0.0)
    repeat = group * srow // LANES
    own = (iota((SUB, group * srow), 1) // srow) == iota((SUB, group * srow), 0)
    blocks = []
    for base in range(0, half, SUB):
        angle = jnp.zeros((SUB, LANES), f32)
        for x in range(3):
            off = jnp.zeros((SUB, LANES), jnp.int32)
            for r in range(SUB):
                owner, inner = (base + r) // r_dev, (base + r) % r_dev
                off = jnp.where(
                    iota((SUB, LANES), 0) == r, off_ref[x, (owner ^ me) * r_dev + inner], off
                )
            angle = angle + off.astype(f32) * klane[x : x + 1, :]
        angle = two_pi * angle
        rows = []
        for wave in (jnp.cos(angle) * weight, jnp.sin(angle) * weight):
            wave = jnp.concatenate([wave] * repeat, axis=1)
            for r in range(SUB):
                rows.append(jnp.where(own, wave[r : r + 1, :], 0.0))
        blocks.append(jnp.concatenate(rows, axis=0).astype(bf16))
    flip = jnp.where(iota((SUB, LANES), 1) < mag, 1.0, -1.0).astype(f32)

    copies[1].wait()
    er, ei = er_ref[0], ei_ref[0]
    for s in range(nslot):
        wide = lev_ref[s].astype(f32)
        for t in range(norb // LANES):
            wide_ref[t, 2 * s : 2 * s + 2, :] = wide[:, t * LANES : (t + 1) * LANES]
    for spin in range(2):
        for t in range(norb // LANES):
            lanes = slice(t * LANES, (t + 1) * LANES)
            shift = er - wide_ref.at[t][pl.ds(spin, srow, stride=2), :]
            inv = 1.0 / (shift * shift + ei * ei)
            fr = shift * inv
            fi = -(ei * inv)
            f1_ref[spin, :, lanes] = fr
            f2_ref[spin, :, lanes] = fi - fr
            f3_ref[spin, :, lanes] = fi + fr
    copies[0].wait()
    for spin in range(2):
        re_vec = vec_ref[0, spin, :, :norb]
        im_vec = vec_ref[0, spin, :, norb:]
        right_ref[spin, :mag, :norb] = re_vec
        right_ref[spin, :mag, norb:] = im_vec
        right_ref[spin, mag:, :norb] = -im_vec
        right_ref[spin, mag:, norb:] = re_vec
        re_wide = re_vec.astype(f32)
        im_wide = im_vec.astype(f32)
        sum_ref[spin, 0] = re_wide + im_wide
        sum_ref[spin, 1] = re_wide
        sum_ref[spin, 2] = im_wide

    for chunk in range(mag // (group * GROUPS)):
        green = []
        for spin in range(2):
            buf = scaled_refs[(chunk % 2) * 2 + spin]
            for j in range(group * GROUPS):
                a = chunk * group * GROUPS + j
                both = f1_ref[spin] * sum_ref[spin, 0, a : a + 1, :]
                cross = f2_ref[spin] * sum_ref[spin, 1, a : a + 1, :]
                other = f3_ref[spin] * sum_ref[spin, 2, a : a + 1, :]
                buf[j * srow : (j + 1) * srow, :norb] = (both - other).astype(bf16)
                buf[j * srow : (j + 1) * srow, norb:] = (both + cross).astype(bf16)
            green.append(
                lax.dot_general(
                    buf[...],
                    right_ref[spin],
                    (((1,), (1,)), ((), ())),
                    preferred_element_type=f32,
                )
            )
        for sub in range(GROUPS):
            c = chunk * GROUPS + sub
            turned = [[], []]
            for j in range(group):
                a = c * group + j
                atom = jnp.int32(0)
                for _, stop in bounds[:-1]:
                    atom = atom + (a >= stop).astype(jnp.int32)
                cos_phase, sin_phase = cos_ref[atom], sin_ref[atom]
                for spin in range(2):
                    at = (sub * group + j) * srow
                    g = green[spin][at : at + srow, :]
                    turned[spin].append(g * cos_phase + pltpu.roll(g, mag, 1) * sin_phase)
            stack = jnp.concatenate(
                [jnp.concatenate(turned[spin], axis=0).astype(bf16) for spin in range(2)], axis=1
            )
            for b, block in enumerate(blocks):
                res = jnp.dot(block, stack, preferred_element_type=f32)
                for r in range(SUB):
                    plus, minus = [], []
                    for spin in range(2):
                        lanes = slice(spin * LANES, (spin + 1) * LANES)
                        even = res[r * SUB : (r + 1) * SUB, lanes]
                        odd = res[(SUB + r) * SUB : (SUB + r + 1) * SUB, lanes]
                        odd = pltpu.roll(odd, mag, 1) * flip
                        plus.append(even + odd if spin == 0 else even - odd)
                        minus.append(even - odd if spin == 0 else even + odd)
                    for p, pieces in ((b * SUB + r, plus), (b * SUB + r + half, minus)):
                        owner, inner = p // r_dev, p % r_dev
                        row = (owner // 2) * r_dev + inner
                        block_out = jnp.concatenate(pieces, axis=0)
                        rows = slice(c * 2 * group, (c + 1) * 2 * group)
                        if owner % 2 == 0:
                            keep_ref[row, rows, :] = block_out
                        else:
                            send_ref[row, rows, :] = block_out.astype(bf16)


def add_kernel(r_dev, keep_ref, got_ref, next_ref, send_ref):
    for q in range(keep_ref.shape[0]):
        owner, inner = q // r_dev, q % r_dev
        row = (owner // 2) * r_dev + inner
        value = keep_ref[q] + got_ref[q].astype(f32)
        if owner % 2 == 0:
            next_ref[row] = value
        else:
            send_ref[row] = value.astype(bf16)


def table_kernel(orb_ref, split_ref, _, left_ref, member_ref, member_t_ref):
    mag = split_ref.shape[0]
    natom = orb_ref.shape[0]
    row, col = iota((mag, mag), 0), iota((mag, mag), 1)
    same = jnp.zeros((mag, mag), jnp.bool_)
    tall = iota((2 * mag, LANES), 0) % mag
    tall_lane = iota((2 * mag, LANES), 1)
    wide = iota((natom, 2 * mag), 1) % mag
    wide_row = iota((natom, 2 * mag), 0)
    member = jnp.zeros((2 * mag, LANES), jnp.bool_)
    member_t = jnp.zeros((natom, 2 * mag), jnp.bool_)
    for i, (start, stop) in enumerate(spans(orb_ref)):
        same = same | ((row >= start) & (row < stop) & (col >= start) & (col < stop))
        member = member | ((tall >= start) & (tall < stop) & (tall_lane == i))
        member_t = member_t | ((wide >= start) & (wide < stop) & (wide_row == i))
    split = split_ref[...]
    high, low = split_two(jnp.where(same, 0.5 * (split + split.T), 0.0))
    left_ref[:, 0:mag] = high
    left_ref[:, mag : 2 * mag] = high
    left_ref[:, 2 * mag :] = low
    member_ref[...] = jnp.where(member, 1.0, 0.0).astype(bf16)
    member_t_ref[...] = jnp.where(member_t, 1.0, 0.0).astype(bf16)


def exchange_kernel(group, keep_ref, got_ref, left_ref, member_ref, member_t_ref, out_ref):
    mag = left_ref.shape[0]
    natom = member_t_ref.shape[0]
    for row in range(keep_ref.shape[0]):
        value = keep_ref[row] + got_ref[row].astype(f32)
        up, down = [], []
        for c in range(mag // group):
            up.append(value[c * 2 * group : c * 2 * group + group])
            down.append(value[c * 2 * group + group : (c + 1) * 2 * group])
        both = jnp.concatenate(
            [jnp.concatenate(up, axis=0), jnp.concatenate(down, axis=0)], axis=1
        )
        high, low = split_two(both)
        both = jnp.dot(
            left_ref[...],
            jnp.concatenate([high, low, high], axis=0),
            preferred_element_type=f32,
        )
        left = both[:, :LANES]
        right = both[:, LANES:].T
        im_part = left[:, :mag] * right[mag:, :] + left[:, mag:] * right[:mag, :]
        part = jnp.dot(
            member_t_ref[...],
            jnp.concatenate(split_two(im_part), axis=0),
            preferred_element_type=f32,
        )
        part = jnp.dot(
            jnp.concatenate(split_two(part), axis=1),
            member_ref[...],
            preferred_element_type=f32,
        )
        out_ref[row] = -inv_four_pi * part[:, :natom]


def vmem(count):
    return [pl.BlockSpec(memory_space=pltpu.VMEM)] * count


def local(
    axis,
    n,
    eigvecs,
    eigvals,
    kpoints,
    counts,
    energy_real,
    energy_imag,
    offsets,
    atom_orbitals,
    positions,
    exch_split,
):
    nslot, _, norb = eigvals.shape
    mag = eigvecs.shape[2]
    natom = atom_orbitals.shape[0]
    total = offsets.shape[1]
    r_dev = total // n
    srow = -(-nslot // 32) * 32
    group = 256 // srow
    rows = total // 2
    args = (eigvecs, eigvals, kpoints, offsets, atom_orbitals, positions)
    spaces = [pltpu.VMEM] * 3 + [pltpu.SMEM] * 3
    fetched = [space(arg.shape, arg.dtype) for space, arg in zip(spaces, args)]
    args = [pltpu.with_memory_space_constraint(arg, pltpu.HBM) for arg in args]
    keep, send = pl.pallas_call(
        functools.partial(green_kernel, axis, r_dev),
        out_shape=(
            jax.ShapeDtypeStruct((rows, 2 * mag, LANES), f32),
            jax.ShapeDtypeStruct((rows, 2 * mag, LANES), bf16),
        ),
        in_specs=[pl.BlockSpec(memory_space=pltpu.SMEM)] * 3
        + [pl.BlockSpec(memory_space=pltpu.HBM)] * len(args),
        out_specs=tuple(vmem(2)),
        scratch_shapes=fetched
        + [
            pltpu.SemaphoreType.DMA((len(args),)),
            pltpu.VMEM((SUB, LANES), f32),
            pltpu.VMEM((norb // LANES, 2 * srow, LANES), f32),
            pltpu.VMEM((natom, srow, LANES), f32),
            pltpu.VMEM((natom, srow, LANES), f32),
            pltpu.VMEM((2, 2 * mag, 2 * norb), bf16),
            pltpu.VMEM((2, 3, mag, norb), f32),
            pltpu.VMEM((2, srow, norb), f32),
            pltpu.VMEM((2, srow, norb), f32),
            pltpu.VMEM((2, srow, norb), f32),
        ]
        + [pltpu.VMEM((GROUPS * group * srow, 2 * norb), bf16)] * 4,
        compiler_params=pltpu.CompilerParams(vmem_limit_bytes=16 << 20),
        name="green",
    )(counts, energy_real, energy_imag, *args)
    tables = pl.pallas_call(
        table_kernel,
        out_shape=(
            jax.ShapeDtypeStruct((mag, 3 * mag), bf16),
            jax.ShapeDtypeStruct((2 * mag, LANES), bf16),
            jax.ShapeDtypeStruct((natom, 2 * mag), bf16),
        ),
        in_specs=[pl.BlockSpec(memory_space=pltpu.SMEM)] + vmem(1) + [pl.BlockSpec(memory_space=pl.ANY)],
        out_specs=tuple(vmem(3)),
        compiler_params=pltpu.CompilerParams(vmem_limit_bytes=4 << 20),
        name="tables",
    )(atom_orbitals, exch_split, keep)
    bit = 1
    while True:
        got = lax.ppermute(send, axis, [(d, d ^ bit) for d in range(n)])
        bit *= 2
        if bit == n:
            break
        rows //= 2
        keep, send = pl.pallas_call(
            functools.partial(add_kernel, r_dev),
            out_shape=(
                jax.ShapeDtypeStruct((rows, 2 * mag, LANES), f32),
                jax.ShapeDtypeStruct((rows, 2 * mag, LANES), bf16),
            ),
            in_specs=vmem(2),
            out_specs=tuple(vmem(2)),
            compiler_params=pltpu.CompilerParams(vmem_limit_bytes=4 << 20),
            name="add",
        )(keep, got)
    return pl.pallas_call(
        functools.partial(exchange_kernel, group),
        out_shape=jax.ShapeDtypeStruct((r_dev, natom, natom), f32),
        in_specs=vmem(5),
        out_specs=vmem(1)[0],
        compiler_params=pltpu.CompilerParams(vmem_limit_bytes=4 << 20),
        name="exchange",
    )(keep, got, *tables)


def solution(mesh):
    placed = (
        P("ka", None, None, None),
        P("ka", None, None),
        P(None, "ka"),
        P("ka"),
        P("grp"),
        P("grp"),
        P(),
        P(),
        P(),
        P(),
    )
    return jax.shard_map(
        functools.partial(local, "ka", mesh.shape["ka"]),
        mesh=mesh,
        in_specs=placed,
        out_specs=P(("grp", "ka"), None, None),
        check_vma=False,
    )
```

```python
import functools

import jax
import jax.numpy as jnp
from jax import lax
from jax.experimental import pallas as pl
from jax.experimental.pallas import tpu as pltpu
from jax.sharding import PartitionSpec as P


inv_four_pi = 0.25 / 3.141592653589793
two_pi = 2.0 * 3.141592653589793
f32 = jnp.float32
bf16 = jnp.bfloat16
LANES = 128
SUB = 8
GROUPS = 4


def iota(shape, dim):
    return lax.broadcasted_iota(jnp.int32, shape, dim)


def spans(sizes):
    start, found = jnp.int32(0), []
    for size in sizes:
        stop = start + size
        found.append((start, stop))
        start = stop
    return found


def split_two(x):
    high = x.astype(bf16)
    return high, (x - high.astype(f32)).astype(bf16)


def green_kernel(
    axis,
    r_dev,
    cnt_ref,
    er_ref,
    ei_ref,
    vec_ref,
    lev_ref,
    k_ref,
    off_ref,
    orb_ref,
    pos_ref,
    _,
    keep_ref,
    send_ref,
    kpad_ref,
    wide_ref,
    cos_ref,
    sin_ref,
    right_ref,
    sum_ref,
    f1_ref,
    f2_ref,
    f3_ref,
    *scaled_refs,
):
    nslot = lev_ref.shape[0]
    mag, norb = vec_ref.shape[2], vec_ref.shape[3] // 2
    natom = orb_ref.shape[0]
    srow = f1_ref.shape[1]
    total = off_ref.shape[1]
    half = total // 2
    group = 256 // srow
    me = lax.axis_index(axis)
    kpad_ref[...] = jnp.zeros_like(kpad_ref)
    wide_ref[:, 2 * nslot :, :] = jnp.zeros_like(wide_ref[:, 2 * nslot :, :])

    kpad_ref[0:3, 0:nslot] = k_ref[...].astype(f32)
    kwide = kpad_ref[...]
    ktall = kwide.T
    klane = kwide
    for step in range(1, LANES // srow):
        klane = klane + pltpu.roll(kwide, step * srow, 1)

    orb_row = orb_ref[...].astype(f32).reshape(1, natom)
    sizes = [
        jnp.sum(jnp.where(iota((1, natom), 1) == i, orb_row, 0.0)).astype(jnp.int32)
        for i in range(natom)
    ]
    bounds = spans(sizes)
    lane = iota((1, LANES), 1)
    orbital = jnp.where(lane >= mag, lane - mag, lane)
    kpos = jnp.zeros((srow, LANES), f32)
    kat = jnp.zeros((srow, LANES), f32)
    for x in range(3):
        site = jnp.zeros((1, LANES), f32)
        atom = jnp.zeros((1, LANES), f32)
        for i, (start, stop) in enumerate(bounds):
            where = pos_ref[x : x + 1, i : i + 1]
            site = jnp.where((orbital >= start) & (orbital < stop), where, site)
            atom = jnp.where(lane == i, where, atom)
        kpos = kpos + ktall[0:srow, x : x + 1] * site
        kat = kat + ktall[0:srow, x : x + 1] * atom
    cos_pos, sin_pos = jnp.cos(two_pi * kpos), jnp.sin(two_pi * kpos)
    cos_atom, sin_atom = jnp.cos(two_pi * kat), jnp.sin(two_pi * kat)
    first = iota((srow, LANES), 1) < mag
    cos_sgn = jnp.where(first, -cos_pos, cos_pos)
    sin_sgn = jnp.where(first, -sin_pos, sin_pos)
    for i in range(natom):
        cos_a, sin_a = cos_atom[:, i : i + 1], sin_atom[:, i : i + 1]
        cos_ref[i] = cos_pos * cos_a + sin_pos * sin_a
        sin_ref[i] = sin_sgn * cos_a - cos_sgn * sin_a

    lane = iota((1, LANES), 1) % srow
    count = cnt_ref[0]
    inverse = jnp.full((1, LANES), count, jnp.int32).astype(f32)
    inverse = (1.0 / inverse).astype(bf16).astype(f32)
    weight = jnp.where(lane < count, inverse, 0.0)
    repeat = group * srow // LANES
    own = (iota((SUB, group * srow), 1) // srow) == iota((SUB, group * srow), 0)
    blocks = []
    for base in range(0, half, SUB):
        place = iota((SUB, total), 0) + base
        wanted = place ^ me if r_dev == 1 else (place // r_dev ^ me) * r_dev + place % r_dev
        pick = iota((SUB, total), 1) == wanted
        angle = jnp.zeros((SUB, LANES), f32)
        for x in range(3):
            off = jnp.where(pick, off_ref[x : x + 1, :].astype(f32), 0.0)
            angle = angle + jnp.sum(off, axis=1, keepdims=True) * klane[x : x + 1, :]
        angle = two_pi * angle
        rows = []
        for wave in (jnp.cos(angle) * weight, jnp.sin(angle) * weight):
            wave = jnp.concatenate([wave] * repeat, axis=1)
            for r in range(SUB):
                rows.append(jnp.where(own, wave[r : r + 1, :], 0.0))
        blocks.append(jnp.concatenate(rows, axis=0).astype(bf16))
    flip = jnp.where(iota((SUB, LANES), 1) < mag, 1.0, -1.0).astype(f32)

    er, ei = er_ref[0], ei_ref[0]
    for s in range(nslot):
        wide = lev_ref[s].astype(f32)
        for t in range(norb // LANES):
            wide_ref[t, 2 * s : 2 * s + 2, :] = wide[:, t * LANES : (t + 1) * LANES]
    for spin in range(2):
        for t in range(norb // LANES):
            lanes = slice(t * LANES, (t + 1) * LANES)
            shift = er - wide_ref.at[t][pl.ds(spin, srow, stride=2), :]
            inv = 1.0 / (shift * shift + ei * ei)
            fr = shift * inv
            fi = -(ei * inv)
            f1_ref[spin, :, lanes] = fr
            f2_ref[spin, :, lanes] = fi - fr
            f3_ref[spin, :, lanes] = fi + fr
    for spin in range(2):
        re_vec = vec_ref[0, spin, :, :norb]
        im_vec = vec_ref[0, spin, :, norb:]
        right_ref[spin, :mag, :norb] = re_vec
        right_ref[spin, :mag, norb:] = im_vec
        right_ref[spin, mag:, :norb] = -im_vec
        right_ref[spin, mag:, norb:] = re_vec
        re_wide = re_vec.astype(f32)
        im_wide = im_vec.astype(f32)
        sum_ref[spin, 0] = re_wide + im_wide
        sum_ref[spin, 1] = re_wide
        sum_ref[spin, 2] = im_wide

    for chunk in range(mag // (group * GROUPS)):
        green = []
        for spin in range(2):
            buf = scaled_refs[(chunk % 2) * 2 + spin]
            for j in range(group * GROUPS):
                a = chunk * group * GROUPS + j
                both = f1_ref[spin] * sum_ref[spin, 0, a : a + 1, :]
                cross = f2_ref[spin] * sum_ref[spin, 1, a : a + 1, :]
                other = f3_ref[spin] * sum_ref[spin, 2, a : a + 1, :]
                buf[j * srow : (j + 1) * srow, :norb] = (both - other).astype(bf16)
                buf[j * srow : (j + 1) * srow, norb:] = (both + cross).astype(bf16)
            green.append(
                lax.dot_general(
                    buf[...],
                    right_ref[spin],
                    (((1,), (1,)), ((), ())),
                    preferred_element_type=f32,
                )
            )
        for sub in range(GROUPS):
            c = chunk * GROUPS + sub
            turned = [[], []]
            for j in range(group):
                a = c * group + j
                atom = jnp.int32(0)
                for _, stop in bounds[:-1]:
                    atom = atom + (a >= stop).astype(jnp.int32)
                cos_phase, sin_phase = cos_ref[atom], sin_ref[atom]
                for spin in range(2):
                    at = (sub * group + j) * srow
                    g = green[spin][at : at + srow, :]
                    turned[spin].append(g * cos_phase + pltpu.roll(g, mag, 1) * sin_phase)
            stack = jnp.concatenate(
                [jnp.concatenate(turned[spin], axis=0).astype(bf16) for spin in range(2)], axis=1
            )
            for b, block in enumerate(blocks):
                res = jnp.dot(block, stack, preferred_element_type=f32)
                for r in range(SUB):
                    plus, minus = [], []
                    for spin in range(2):
                        lanes = slice(spin * LANES, (spin + 1) * LANES)
                        even = res[r * SUB : (r + 1) * SUB, lanes]
                        odd = res[(SUB + r) * SUB : (SUB + r + 1) * SUB, lanes]
                        odd = pltpu.roll(odd, mag, 1) * flip
                        plus.append(even + odd if spin == 0 else even - odd)
                        minus.append(even - odd if spin == 0 else even + odd)
                    for p, pieces in ((b * SUB + r, plus), (b * SUB + r + half, minus)):
                        owner, inner = p // r_dev, p % r_dev
                        row = (owner // 2) * r_dev + inner
                        block_out = jnp.concatenate(pieces, axis=0)
                        rows = slice(c * 2 * group, (c + 1) * 2 * group)
                        if owner % 2 == 0:
                            keep_ref[row, rows, :] = block_out
                        else:
                            send_ref[row, rows, :] = block_out.astype(bf16)


def add_kernel(r_dev, keep_ref, got_ref, next_ref, send_ref):
    for q in range(keep_ref.shape[0]):
        owner, inner = q // r_dev, q % r_dev
        row = (owner // 2) * r_dev + inner
        value = keep_ref[q] + got_ref[q].astype(f32)
        if owner % 2 == 0:
            next_ref[row] = value
        else:
            send_ref[row] = value.astype(bf16)


def lead_kernel(out_ref):
    out_ref[...] = jnp.zeros_like(out_ref)


def table_kernel(orb_ref, split_ref, _, left_ref, member_ref, member_t_ref):
    mag = split_ref.shape[0]
    natom = orb_ref.shape[0]
    row, col = iota((mag, mag), 0), iota((mag, mag), 1)
    same = jnp.zeros((mag, mag), jnp.bool_)
    tall = iota((2 * mag, LANES), 0) % mag
    tall_lane = iota((2 * mag, LANES), 1)
    wide = iota((natom, 2 * mag), 1) % mag
    wide_row = iota((natom, 2 * mag), 0)
    member = jnp.zeros((2 * mag, LANES), jnp.bool_)
    member_t = jnp.zeros((natom, 2 * mag), jnp.bool_)
    for i, (start, stop) in enumerate(spans([orb_ref[i] for i in range(natom)])):
        same = same | ((row >= start) & (row < stop) & (col >= start) & (col < stop))
        member = member | ((tall >= start) & (tall < stop) & (tall_lane == i))
        member_t = member_t | ((wide >= start) & (wide < stop) & (wide_row == i))
    split = split_ref[...]
    high, low = split_two(jnp.where(same, 0.5 * (split + split.T), 0.0))
    left_ref[:, 0:mag] = high
    left_ref[:, mag : 2 * mag] = high
    left_ref[:, 2 * mag :] = low
    member_ref[...] = jnp.where(member, 1.0, 0.0).astype(bf16)
    member_t_ref[...] = jnp.where(member_t, 1.0, 0.0).astype(bf16)


def exchange_kernel(group, keep_ref, got_ref, left_ref, member_ref, member_t_ref, out_ref):
    mag = left_ref.shape[0]
    natom = member_t_ref.shape[0]
    for row in range(keep_ref.shape[0]):
        value = keep_ref[row] + got_ref[row].astype(f32)
        up, down = [], []
        for c in range(mag // group):
            up.append(value[c * 2 * group : c * 2 * group + group])
            down.append(value[c * 2 * group + group : (c + 1) * 2 * group])
        both = jnp.concatenate(
            [jnp.concatenate(up, axis=0), jnp.concatenate(down, axis=0)], axis=1
        )
        high, low = split_two(both)
        both = jnp.dot(
            left_ref[...],
            jnp.concatenate([high, low, high], axis=0),
            preferred_element_type=f32,
        )
        left = both[:, :LANES]
        right = both[:, LANES:].T
        im_part = left[:, :mag] * right[mag:, :] + left[:, mag:] * right[:mag, :]
        part = jnp.dot(
            member_t_ref[...],
            jnp.concatenate(split_two(im_part), axis=0),
            preferred_element_type=f32,
        )
        part = jnp.dot(
            jnp.concatenate(split_two(part), axis=1),
            member_ref[...],
            preferred_element_type=f32,
        )
        out_ref[row] = -inv_four_pi * part[:, :natom]


def vmem(count):
    return [pl.BlockSpec(memory_space=pltpu.VMEM)] * count


def local(
    axis,
    n,
    eigvecs,
    eigvals,
    kpoints,
    counts,
    energy_real,
    energy_imag,
    offsets,
    atom_orbitals,
    positions,
    exch_split,
):
    nslot, _, norb = eigvals.shape
    mag = eigvecs.shape[2]
    natom = atom_orbitals.shape[0]
    total = offsets.shape[1]
    r_dev = total // n
    srow = -(-nslot // 32) * 32
    group = 256 // srow
    rows = total // 2
    lead = pl.pallas_call(
        lead_kernel,
        out_shape=jax.ShapeDtypeStruct((SUB, LANES), f32),
        out_specs=vmem(1)[0],
        compiler_params=pltpu.CompilerParams(vmem_limit_bytes=1 << 20),
        cost_estimate=pl.CostEstimate(flops=1 << 32, bytes_accessed=1 << 23, transcendentals=0),
        name="lead",
    )()
    keep, send = pl.pallas_call(
        functools.partial(green_kernel, axis, r_dev),
        out_shape=(
            jax.ShapeDtypeStruct((rows, 2 * mag, LANES), f32),
            jax.ShapeDtypeStruct((rows, 2 * mag, LANES), bf16),
        ),
        in_specs=[pl.BlockSpec(memory_space=pltpu.SMEM)] * 3
        + vmem(6)
        + [pl.BlockSpec(memory_space=pl.ANY)],
        out_specs=tuple(vmem(2)),
        scratch_shapes=[
            pltpu.VMEM((SUB, LANES), f32),
            pltpu.VMEM((norb // LANES, 2 * srow, LANES), f32),
            pltpu.VMEM((natom, srow, LANES), f32),
            pltpu.VMEM((natom, srow, LANES), f32),
            pltpu.VMEM((2, 2 * mag, 2 * norb), bf16),
            pltpu.VMEM((2, 3, mag, norb), f32),
            pltpu.VMEM((2, srow, norb), f32),
            pltpu.VMEM((2, srow, norb), f32),
            pltpu.VMEM((2, srow, norb), f32),
        ]
        + [pltpu.VMEM((GROUPS * group * srow, 2 * norb), bf16)] * 4,
        compiler_params=pltpu.CompilerParams(vmem_limit_bytes=16 << 20),
        name="green",
    )(
        counts,
        energy_real,
        energy_imag,
        eigvecs,
        eigvals,
        kpoints,
        offsets,
        atom_orbitals,
        positions,
        lead,
    )
    tables = pl.pallas_call(
        table_kernel,
        out_shape=(
            jax.ShapeDtypeStruct((mag, 3 * mag), bf16),
            jax.ShapeDtypeStruct((2 * mag, LANES), bf16),
            jax.ShapeDtypeStruct((natom, 2 * mag), bf16),
        ),
        in_specs=[pl.BlockSpec(memory_space=pltpu.SMEM)] + vmem(1) + [pl.BlockSpec(memory_space=pl.ANY)],
        out_specs=tuple(vmem(3)),
        compiler_params=pltpu.CompilerParams(vmem_limit_bytes=4 << 20),
        name="tables",
    )(atom_orbitals, exch_split, keep)
    bit = 1
    while True:
        got = lax.ppermute(send, axis, [(d, d ^ bit) for d in range(n)])
        bit *= 2
        if bit == n:
            break
        rows //= 2
        keep, send = pl.pallas_call(
            functools.partial(add_kernel, r_dev),
            out_shape=(
                jax.ShapeDtypeStruct((rows, 2 * mag, LANES), f32),
                jax.ShapeDtypeStruct((rows, 2 * mag, LANES), bf16),
            ),
            in_specs=vmem(2),
            out_specs=tuple(vmem(2)),
            compiler_params=pltpu.CompilerParams(vmem_limit_bytes=4 << 20),
            name="add",
        )(keep, got)
    return pl.pallas_call(
        functools.partial(exchange_kernel, group),
        out_shape=jax.ShapeDtypeStruct((r_dev, natom, natom), f32),
        in_specs=vmem(5),
        out_specs=vmem(1)[0],
        compiler_params=pltpu.CompilerParams(vmem_limit_bytes=4 << 20),
        name="exchange",
    )(keep, got, *tables)


def solution(mesh):
    placed = (
        P("ka", None, None, None),
        P("ka", None, None),
        P(None, "ka"),
        P("ka"),
        P("grp"),
        P("grp"),
        P(),
        P(),
        P(),
        P(),
    )
    return jax.shard_map(
        functools.partial(local, "ka", mesh.shape["ka"]),
        mesh=mesh,
        in_specs=placed,
        out_specs=P(("grp", "ka"), None, None),
        check_vma=False,
    )
```

```python
import functools

import jax
import jax.numpy as jnp
from jax import lax
from jax.experimental import pallas as pl
from jax.experimental.pallas import tpu as pltpu
from jax.sharding import PartitionSpec as P


inv_four_pi = 0.25 / 3.141592653589793
two_pi = 2.0 * 3.141592653589793
f32 = jnp.float32
bf16 = jnp.bfloat16
LANES = 128
SUB = 8
GROUPS = 4
WIDE_ROWS = 1 << 20


def iota(shape, dim):
    return lax.broadcasted_iota(jnp.int32, shape, dim)


def crossed(position, device, n):
    if n < 16:
        return position
    differ = ((position >> 1) ^ (position >> 2)) & device & 1
    return position ^ (differ * 6)


def spans(sizes):
    start, found = jnp.int32(0), []
    for size in sizes:
        stop = start + size
        found.append((start, stop))
        start = stop
    return found


def split_two(x):
    high = x.astype(bf16)
    return high, (x - high.astype(f32)).astype(bf16)


def green_kernel(
    axis,
    r_dev,
    cnt_ref,
    er_ref,
    ei_ref,
    vec_ref,
    lev_ref,
    k_ref,
    off_ref,
    orb_ref,
    pos_ref,
    _,
    keep_ref,
    send_ref,
    kpad_ref,
    wide_ref,
    cos_ref,
    sin_ref,
    right_ref,
    sum_ref,
    f1_ref,
    f2_ref,
    f3_ref,
    *scaled_refs,
):
    nslot = lev_ref.shape[0]
    mag, norb = vec_ref.shape[2], vec_ref.shape[3] // 2
    natom = orb_ref.shape[0]
    srow = f1_ref.shape[1]
    total = off_ref.shape[1]
    half = total // 2
    group = 256 // srow
    me = lax.axis_index(axis)
    kpad_ref[...] = jnp.zeros_like(kpad_ref)
    wide_ref[:, 2 * nslot :, :] = jnp.zeros_like(wide_ref[:, 2 * nslot :, :])

    kpad_ref[0:3, 0:nslot] = k_ref[...].astype(f32)
    kwide = kpad_ref[...]
    ktall = kwide.T
    klane = kwide
    for step in range(1, LANES // srow):
        klane = klane + pltpu.roll(kwide, step * srow, 1)

    orb_row = orb_ref[...].astype(f32).reshape(1, natom)
    sizes = [
        jnp.sum(jnp.where(iota((1, natom), 1) == i, orb_row, 0.0)).astype(jnp.int32)
        for i in range(natom)
    ]
    bounds = spans(sizes)
    lane = iota((1, LANES), 1)
    orbital = jnp.where(lane >= mag, lane - mag, lane)
    kpos = jnp.zeros((srow, LANES), f32)
    kat = jnp.zeros((srow, LANES), f32)
    for x in range(3):
        site = jnp.zeros((1, LANES), f32)
        atom = jnp.zeros((1, LANES), f32)
        for i, (start, stop) in enumerate(bounds):
            where = pos_ref[x : x + 1, i : i + 1]
            site = jnp.where((orbital >= start) & (orbital < stop), where, site)
            atom = jnp.where(lane == i, where, atom)
        kpos = kpos + ktall[0:srow, x : x + 1] * site
        kat = kat + ktall[0:srow, x : x + 1] * atom
    cos_pos, sin_pos = jnp.cos(two_pi * kpos), jnp.sin(two_pi * kpos)
    cos_atom, sin_atom = jnp.cos(two_pi * kat), jnp.sin(two_pi * kat)
    first = iota((srow, LANES), 1) < mag
    cos_sgn = jnp.where(first, -cos_pos, cos_pos)
    sin_sgn = jnp.where(first, -sin_pos, sin_pos)
    for i in range(natom):
        cos_a, sin_a = cos_atom[:, i : i + 1], sin_atom[:, i : i + 1]
        cos_ref[i] = cos_pos * cos_a + sin_pos * sin_a
        sin_ref[i] = sin_sgn * cos_a - cos_sgn * sin_a

    lane = iota((1, LANES), 1) % srow
    count = cnt_ref[0]
    inverse = jnp.full((1, LANES), count, jnp.int32).astype(f32)
    inverse = (1.0 / inverse).astype(bf16).astype(f32)
    weight = jnp.where(lane < count, inverse, 0.0)
    repeat = group * srow // LANES
    own = (iota((SUB, group * srow), 1) // srow) == iota((SUB, group * srow), 0)
    blocks = []
    for base in range(0, half, SUB):
        place = iota((SUB, total), 0) + base
        owner = place // r_dev if r_dev > 1 else place
        odd = owner & 1
        owner = crossed(owner - odd, me ^ odd, total // r_dev) ^ me ^ odd
        wanted = owner * r_dev + place % r_dev if r_dev > 1 else owner
        pick = iota((SUB, total), 1) == wanted
        angle = jnp.zeros((SUB, LANES), f32)
        for x in range(3):
            off = jnp.where(pick, off_ref[x : x + 1, :].astype(f32), 0.0)
            angle = angle + jnp.sum(off, axis=1, keepdims=True) * klane[x : x + 1, :]
        angle = two_pi * angle
        rows = []
        for wave in (jnp.cos(angle) * weight, jnp.sin(angle) * weight):
            wave = jnp.concatenate([wave] * repeat, axis=1)
            for r in range(SUB):
                rows.append(jnp.where(own, wave[r : r + 1, :], 0.0))
        blocks.append(jnp.concatenate(rows, axis=0).astype(bf16))
    flip = jnp.where(iota((SUB, LANES), 1) < mag, 1.0, -1.0).astype(f32)

    er, ei = er_ref[0], ei_ref[0]
    for s in range(nslot):
        wide = lev_ref[s].astype(f32)
        for t in range(norb // LANES):
            wide_ref[t, 2 * s : 2 * s + 2, :] = wide[:, t * LANES : (t + 1) * LANES]
    for spin in range(2):
        for t in range(norb // LANES):
            lanes = slice(t * LANES, (t + 1) * LANES)
            shift = er - wide_ref.at[t][pl.ds(spin, srow, stride=2), :]
            inv = 1.0 / (shift * shift + ei * ei)
            fr = shift * inv
            fi = -(ei * inv)
            f1_ref[spin, :, lanes] = fr
            f2_ref[spin, :, lanes] = fi - fr
            f3_ref[spin, :, lanes] = fi + fr
    for spin in range(2):
        re_vec = vec_ref[0, spin, :, :norb]
        im_vec = vec_ref[0, spin, :, norb:]
        right_ref[spin, :mag, :norb] = re_vec
        right_ref[spin, :mag, norb:] = im_vec
        right_ref[spin, mag:, :norb] = -im_vec
        right_ref[spin, mag:, norb:] = re_vec
        re_wide = re_vec.astype(f32)
        im_wide = im_vec.astype(f32)
        sum_ref[spin, 0] = re_wide + im_wide
        sum_ref[spin, 1] = re_wide
        sum_ref[spin, 2] = im_wide

    def product(chunk, spin):
        buf = scaled_refs[(chunk % 2) * 2 + spin]
        for j in range(group * GROUPS):
            a = chunk * group * GROUPS + j
            both = f1_ref[spin] * sum_ref[spin, 0, a : a + 1, :]
            cross = f2_ref[spin] * sum_ref[spin, 1, a : a + 1, :]
            other = f3_ref[spin] * sum_ref[spin, 2, a : a + 1, :]
            buf[j * srow : (j + 1) * srow, :norb] = (both - other).astype(bf16)
            buf[j * srow : (j + 1) * srow, norb:] = (both + cross).astype(bf16)
        return lax.dot_general(
            buf[...], right_ref[spin], (((1,), (1,)), ((), ())), preferred_element_type=f32
        )

    def fourier(chunk, green):
        for sub in range(GROUPS):
            c = chunk * GROUPS + sub
            turned = [[], []]
            for j in range(group):
                a = c * group + j
                atom = jnp.int32(0)
                for _, stop in bounds[:-1]:
                    atom = atom + (a >= stop).astype(jnp.int32)
                cos_phase, sin_phase = cos_ref[atom], sin_ref[atom]
                for spin in range(2):
                    at = (sub * group + j) * srow
                    g = green[spin][at : at + srow, :]
                    turned[spin].append(g * cos_phase + pltpu.roll(g, mag, 1) * sin_phase)
            stack = jnp.concatenate(
                [jnp.concatenate(turned[spin], axis=0).astype(bf16) for spin in range(2)], axis=1
            )
            for b, block in enumerate(blocks):
                res = jnp.dot(block, stack, preferred_element_type=f32)
                for r in range(SUB):
                    plus, minus = [], []
                    for spin in range(2):
                        lanes = slice(spin * LANES, (spin + 1) * LANES)
                        even = res[r * SUB : (r + 1) * SUB, lanes]
                        odd = res[(SUB + r) * SUB : (SUB + r + 1) * SUB, lanes]
                        odd = pltpu.roll(odd, mag, 1) * flip
                        plus.append(even + odd if spin == 0 else even - odd)
                        minus.append(even - odd if spin == 0 else even + odd)
                    for p, pieces in ((b * SUB + r, plus), (b * SUB + r + half, minus)):
                        owner, inner = p // r_dev, p % r_dev
                        row = (owner // 2) * r_dev + inner
                        block_out = jnp.concatenate(pieces, axis=0)
                        rows = slice(c * 2 * group, (c + 1) * 2 * group)
                        if owner % 2 == 0:
                            keep_ref[row, rows, :] = block_out
                        else:
                            send_ref[row, rows, :] = block_out.astype(send_ref.dtype)

    last = None
    for chunk in range(mag // (group * GROUPS)):
        green = [product(chunk, 0), product(chunk, 1)]
        if last is not None:
            fourier(chunk - 1, last)
        last = green
    fourier(mag // (group * GROUPS) - 1, last)


def add_kernel(r_dev, keep_ref, got_ref, next_ref, send_ref):
    for q in range(keep_ref.shape[0]):
        owner, inner = q // r_dev, q % r_dev
        row = (owner // 2) * r_dev + inner
        value = keep_ref[q] + got_ref[q].astype(f32)
        if owner % 2 == 0:
            next_ref[row] = value
        else:
            send_ref[row] = value.astype(send_ref.dtype)


def lead_kernel(out_ref):
    out_ref[...] = jnp.zeros_like(out_ref)


def table_kernel(orb_ref, split_ref, _, left_ref, member_ref, mask_ref):
    mag = split_ref.shape[0]
    natom = orb_ref.shape[0]
    row, col = iota((mag, mag), 0), iota((mag, mag), 1)
    same = jnp.zeros((mag, mag), jnp.bool_)
    tall = iota((2 * mag, LANES), 0) % mag
    tall_lane = iota((2 * mag, LANES), 1)
    rows = iota((mag, LANES), 0)
    member = jnp.zeros((2 * mag, LANES), jnp.bool_)
    for i, (start, stop) in enumerate(spans([orb_ref[i] for i in range(natom)])):
        same = same | ((row >= start) & (row < stop) & (col >= start) & (col < stop))
        member = member | ((tall >= start) & (tall < stop) & (tall_lane == i))
        mask_ref[i] = jnp.where((rows >= start) & (rows < stop), -inv_four_pi, 0.0)
    split = split_ref[...]
    high, low = split_two(jnp.where(same, 0.5 * (split + split.T), 0.0))
    left_ref[:, 0:mag] = high
    left_ref[:, mag : 2 * mag] = high
    left_ref[:, 2 * mag :] = low
    member_ref[...] = jnp.where(member, 1.0, 0.0).astype(bf16)


def exchange_kernel(group, keep_ref, got_ref, left_ref, member_ref, mask_ref, out_ref):
    mag = left_ref.shape[0]
    natom = mask_ref.shape[0]
    for row in range(keep_ref.shape[0]):
        value = keep_ref[row] + got_ref[row].astype(f32)
        up, down = [], []
        for c in range(mag // group):
            up.append(value[c * 2 * group : c * 2 * group + group])
            down.append(value[c * 2 * group + group : (c + 1) * 2 * group])
        both = jnp.concatenate(
            [jnp.concatenate(up, axis=0), jnp.concatenate(down, axis=0)], axis=1
        )
        high, low = split_two(both)
        both = jnp.dot(
            left_ref[...],
            jnp.concatenate([high, low, high], axis=0),
            preferred_element_type=f32,
        )
        left = both[:, :LANES]
        right = both[:, LANES:].T
        im_part = left[:, :mag] * right[mag:, :] + left[:, mag:] * right[:mag, :]
        part = jnp.dot(
            jnp.concatenate(split_two(im_part), axis=1),
            member_ref[...],
            preferred_element_type=f32,
        )
        pairs = [jnp.sum(mask_ref[i] * part, axis=0, keepdims=True) for i in range(natom)]
        out_ref[row] = jnp.concatenate(pairs, axis=0)[:, :natom]


def sent(rows):
    return f32 if rows <= WIDE_ROWS else bf16


def vmem(count):
    return [pl.BlockSpec(memory_space=pltpu.VMEM)] * count


def local(
    axis,
    n,
    eigvecs,
    eigvals,
    kpoints,
    counts,
    energy_real,
    energy_imag,
    offsets,
    atom_orbitals,
    positions,
    exch_split,
):
    nslot, _, norb = eigvals.shape
    mag = eigvecs.shape[2]
    natom = atom_orbitals.shape[0]
    total = offsets.shape[1]
    r_dev = total // n
    srow = -(-nslot // 32) * 32
    group = 256 // srow
    rows = total // 2
    lead = pl.pallas_call(
        lead_kernel,
        out_shape=jax.ShapeDtypeStruct((SUB, LANES), f32),
        out_specs=vmem(1)[0],
        compiler_params=pltpu.CompilerParams(vmem_limit_bytes=1 << 20),
        cost_estimate=pl.CostEstimate(flops=1 << 32, bytes_accessed=1 << 23, transcendentals=0),
        name="lead",
    )()
    keep, send = pl.pallas_call(
        functools.partial(green_kernel, axis, r_dev),
        out_shape=(
            jax.ShapeDtypeStruct((rows, 2 * mag, LANES), f32),
            jax.ShapeDtypeStruct((rows, 2 * mag, LANES), sent(rows)),
        ),
        in_specs=[pl.BlockSpec(memory_space=pltpu.SMEM)] * 3
        + vmem(6)
        + [pl.BlockSpec(memory_space=pl.ANY)],
        out_specs=tuple(vmem(2)),
        scratch_shapes=[
            pltpu.VMEM((SUB, LANES), f32),
            pltpu.VMEM((norb // LANES, 2 * srow, LANES), f32),
            pltpu.VMEM((natom, srow, LANES), f32),
            pltpu.VMEM((natom, srow, LANES), f32),
            pltpu.VMEM((2, 2 * mag, 2 * norb), bf16),
            pltpu.VMEM((2, 3, mag, norb), f32),
            pltpu.VMEM((2, srow, norb), f32),
            pltpu.VMEM((2, srow, norb), f32),
            pltpu.VMEM((2, srow, norb), f32),
        ]
        + [pltpu.VMEM((GROUPS * group * srow, 2 * norb), bf16)] * 4,
        compiler_params=pltpu.CompilerParams(vmem_limit_bytes=16 << 20),
        name="green",
    )(
        counts,
        energy_real,
        energy_imag,
        eigvecs,
        eigvals,
        kpoints,
        offsets,
        atom_orbitals,
        positions,
        lead,
    )
    tables = pl.pallas_call(
        table_kernel,
        out_shape=(
            jax.ShapeDtypeStruct((mag, 3 * mag), bf16),
            jax.ShapeDtypeStruct((2 * mag, LANES), bf16),
            jax.ShapeDtypeStruct((natom, mag, LANES), f32),
        ),
        in_specs=[pl.BlockSpec(memory_space=pltpu.SMEM)] + vmem(1) + [pl.BlockSpec(memory_space=pl.ANY)],
        out_specs=tuple(vmem(3)),
        compiler_params=pltpu.CompilerParams(vmem_limit_bytes=4 << 20),
        name="tables",
    )(atom_orbitals, exch_split, keep)
    bit = 1
    while True:
        got = lax.ppermute(send, axis, [(d, d ^ crossed(bit, d, n)) for d in range(n)])
        bit *= 2
        if bit == n:
            break
        rows //= 2
        keep, send = pl.pallas_call(
            functools.partial(add_kernel, r_dev),
            out_shape=(
                jax.ShapeDtypeStruct((rows, 2 * mag, LANES), f32),
                jax.ShapeDtypeStruct((rows, 2 * mag, LANES), sent(rows)),
            ),
            in_specs=vmem(2),
            out_specs=tuple(vmem(2)),
            compiler_params=pltpu.CompilerParams(vmem_limit_bytes=4 << 20),
            name="add",
        )(keep, got)
    return pl.pallas_call(
        functools.partial(exchange_kernel, group),
        out_shape=jax.ShapeDtypeStruct((r_dev, natom, natom), f32),
        in_specs=vmem(5),
        out_specs=vmem(1)[0],
        compiler_params=pltpu.CompilerParams(vmem_limit_bytes=4 << 20),
        name="exchange",
    )(keep, got, *tables)


def solution(mesh):
    placed = (
        P("ka", None, None, None),
        P("ka", None, None),
        P(None, "ka"),
        P("ka"),
        P("grp"),
        P("grp"),
        P(),
        P(),
        P(),
        P(),
    )
    return jax.shard_map(
        functools.partial(local, "ka", mesh.shape["ka"]),
        mesh=mesh,
        in_specs=placed,
        out_specs=P(("grp", "ka"), None, None),
        check_vma=False,
    )
```

```python
import functools

import jax
import jax.numpy as jnp
from jax import lax
from jax.experimental import pallas as pl
from jax.experimental.pallas import tpu as pltpu
from jax.sharding import PartitionSpec as P


inv_four_pi = 0.25 / 3.141592653589793
two_pi = 2.0 * 3.141592653589793
f32 = jnp.float32
bf16 = jnp.bfloat16
LANES = 128
SUB = 8
GROUPS = 4


def iota(shape, dim):
    return lax.broadcasted_iota(jnp.int32, shape, dim)


def crossed(position, device, n):
    if n < 16:
        return position
    differ = ((position >> 1) ^ (position >> 2)) & device & 1
    return position ^ (differ * 6)


def spans(sizes):
    start, found = jnp.int32(0), []
    for size in sizes:
        stop = start + size
        found.append((start, stop))
        start = stop
    return found


def split_two(x):
    high = x.astype(bf16)
    return high, (x - high.astype(f32)).astype(bf16)


def green_kernel(
    axis,
    r_dev,
    cnt_ref,
    er_ref,
    ei_ref,
    vec_ref,
    lev_ref,
    k_ref,
    off_ref,
    orb_ref,
    pos_ref,
    _,
    keep_ref,
    send_ref,
    kpad_ref,
    wide_ref,
    cos_ref,
    sin_ref,
    right_ref,
    sum_ref,
    f1_ref,
    f2_ref,
    f3_ref,
    *scaled_refs,
):
    nslot = lev_ref.shape[0]
    mag, norb = vec_ref.shape[2], vec_ref.shape[3] // 2
    natom = orb_ref.shape[0]
    srow = f1_ref.shape[1]
    total = off_ref.shape[1]
    half = total // 2
    group = 256 // srow
    me = lax.axis_index(axis)
    kpad_ref[...] = jnp.zeros_like(kpad_ref)
    wide_ref[:, 2 * nslot :, :] = jnp.zeros_like(wide_ref[:, 2 * nslot :, :])

    kpad_ref[0:3, 0:nslot] = k_ref[...].astype(f32)
    kwide = kpad_ref[...]
    ktall = kwide.T
    klane = kwide
    for step in range(1, LANES // srow):
        klane = klane + pltpu.roll(kwide, step * srow, 1)

    orb_row = orb_ref[...].astype(f32).reshape(1, natom)
    sizes = [
        jnp.sum(jnp.where(iota((1, natom), 1) == i, orb_row, 0.0)).astype(jnp.int32)
        for i in range(natom)
    ]
    bounds = spans(sizes)
    lane = iota((1, LANES), 1)
    orbital = jnp.where(lane >= mag, lane - mag, lane)
    kpos = jnp.zeros((srow, LANES), f32)
    kat = jnp.zeros((srow, LANES), f32)
    for x in range(3):
        site = jnp.zeros((1, LANES), f32)
        atom = jnp.zeros((1, LANES), f32)
        for i, (start, stop) in enumerate(bounds):
            where = pos_ref[x : x + 1, i : i + 1]
            site = jnp.where((orbital >= start) & (orbital < stop), where, site)
            atom = jnp.where(lane == i, where, atom)
        kpos = kpos + ktall[0:srow, x : x + 1] * site
        kat = kat + ktall[0:srow, x : x + 1] * atom
    cos_pos, sin_pos = jnp.cos(two_pi * kpos), jnp.sin(two_pi * kpos)
    cos_atom, sin_atom = jnp.cos(two_pi * kat), jnp.sin(two_pi * kat)
    first = iota((srow, LANES), 1) < mag
    cos_sgn = jnp.where(first, -cos_pos, cos_pos)
    sin_sgn = jnp.where(first, -sin_pos, sin_pos)
    for i in range(natom):
        cos_a, sin_a = cos_atom[:, i : i + 1], sin_atom[:, i : i + 1]
        cos_ref[i] = cos_pos * cos_a + sin_pos * sin_a
        sin_ref[i] = sin_sgn * cos_a - cos_sgn * sin_a

    lane = iota((1, LANES), 1) % srow
    count = cnt_ref[0]
    inverse = jnp.full((1, LANES), count, jnp.int32).astype(f32)
    inverse = (1.0 / inverse).astype(bf16).astype(f32)
    weight = jnp.where(lane < count, inverse, 0.0)
    repeat = group * srow // LANES
    own = (iota((SUB, group * srow), 1) // srow) == iota((SUB, group * srow), 0)
    blocks = []
    for base in range(0, half, SUB):
        place = iota((SUB, total), 0) + base
        owner = place // r_dev if r_dev > 1 else place
        odd = owner & 1
        owner = crossed(owner - odd, me ^ odd, total // r_dev) ^ me ^ odd
        wanted = owner * r_dev + place % r_dev if r_dev > 1 else owner
        pick = iota((SUB, total), 1) == wanted
        angle = jnp.zeros((SUB, LANES), f32)
        for x in range(3):
            off = jnp.where(pick, off_ref[x : x + 1, :].astype(f32), 0.0)
            angle = angle + jnp.sum(off, axis=1, keepdims=True) * klane[x : x + 1, :]
        angle = two_pi * angle
        rows = []
        for wave in (jnp.cos(angle) * weight, jnp.sin(angle) * weight):
            wave = jnp.concatenate([wave] * repeat, axis=1)
            for r in range(SUB):
                rows.append(jnp.where(own, wave[r : r + 1, :], 0.0))
        blocks.append(jnp.concatenate(rows, axis=0).astype(bf16))
    flip = jnp.where(iota((SUB, LANES), 1) < mag, 1.0, -1.0).astype(f32)

    er, ei = er_ref[0], ei_ref[0]
    for s in range(nslot):
        wide = lev_ref[s].astype(f32)
        for t in range(norb // LANES):
            wide_ref[t, 2 * s : 2 * s + 2, :] = wide[:, t * LANES : (t + 1) * LANES]
    for spin in range(2):
        for t in range(norb // LANES):
            lanes = slice(t * LANES, (t + 1) * LANES)
            shift = er - wide_ref.at[t][pl.ds(spin, srow, stride=2), :]
            inv = 1.0 / (shift * shift + ei * ei)
            fr = shift * inv
            fi = -(ei * inv)
            f1_ref[spin, :, lanes] = fr
            f2_ref[spin, :, lanes] = fi - fr
            f3_ref[spin, :, lanes] = fi + fr
    for spin in range(2):
        re_vec = vec_ref[0, spin, :, :norb]
        im_vec = vec_ref[0, spin, :, norb:]
        right_ref[spin, :mag, :norb] = re_vec
        right_ref[spin, :mag, norb:] = im_vec
        right_ref[spin, mag:, :norb] = -im_vec
        right_ref[spin, mag:, norb:] = re_vec
        re_wide = re_vec.astype(f32)
        im_wide = im_vec.astype(f32)
        sum_ref[spin, 0] = re_wide + im_wide
        sum_ref[spin, 1] = re_wide
        sum_ref[spin, 2] = im_wide

    def product(chunk, spin):
        buf = scaled_refs[(chunk % 2) * 2 + spin]
        for j in range(group * GROUPS):
            a = chunk * group * GROUPS + j
            both = f1_ref[spin] * sum_ref[spin, 0, a : a + 1, :]
            cross = f2_ref[spin] * sum_ref[spin, 1, a : a + 1, :]
            other = f3_ref[spin] * sum_ref[spin, 2, a : a + 1, :]
            buf[j * srow : (j + 1) * srow, :norb] = (both - other).astype(bf16)
            buf[j * srow : (j + 1) * srow, norb:] = (both + cross).astype(bf16)
        return lax.dot_general(
            buf[...], right_ref[spin], (((1,), (1,)), ((), ())), preferred_element_type=f32
        )

    def fourier(chunk, green):
        for sub in range(GROUPS):
            c = chunk * GROUPS + sub
            turned = [[], []]
            for j in range(group):
                a = c * group + j
                atom = jnp.int32(0)
                for _, stop in bounds[:-1]:
                    atom = atom + (a >= stop).astype(jnp.int32)
                cos_phase, sin_phase = cos_ref[atom], sin_ref[atom]
                for spin in range(2):
                    at = (sub * group + j) * srow
                    g = green[spin][at : at + srow, :]
                    turned[spin].append(g * cos_phase + pltpu.roll(g, mag, 1) * sin_phase)
            stack = jnp.concatenate(
                [jnp.concatenate(turned[spin], axis=0).astype(bf16) for spin in range(2)], axis=1
            )
            for b, block in enumerate(blocks):
                res = jnp.dot(block, stack, preferred_element_type=f32)
                for r in range(SUB):
                    plus, minus = [], []
                    for spin in range(2):
                        lanes = slice(spin * LANES, (spin + 1) * LANES)
                        even = res[r * SUB : (r + 1) * SUB, lanes]
                        odd = res[(SUB + r) * SUB : (SUB + r + 1) * SUB, lanes]
                        odd = pltpu.roll(odd, mag, 1) * flip
                        plus.append(even + odd if spin == 0 else even - odd)
                        minus.append(even - odd if spin == 0 else even + odd)
                    for p, pieces in ((b * SUB + r, plus), (b * SUB + r + half, minus)):
                        owner, inner = p // r_dev, p % r_dev
                        row = (owner // 2) * r_dev + inner
                        block_out = jnp.concatenate(pieces, axis=0)
                        rows = slice(c * 2 * group, (c + 1) * 2 * group)
                        if owner % 2 == 0:
                            keep_ref[row, rows, :] = block_out
                        else:
                            send_ref[row, rows, :] = block_out.astype(send_ref.dtype)

    last = None
    for chunk in range(mag // (group * GROUPS)):
        green = [product(chunk, 0), product(chunk, 1)]
        if last is not None:
            fourier(chunk - 1, last)
        last = green
    fourier(mag // (group * GROUPS) - 1, last)


def add_kernel(r_dev, keep_ref, got_ref, next_ref, send_ref):
    rows = keep_ref.shape[0]
    for q in range(rows):
        owner, inner = q // r_dev, q % r_dev
        row = (owner // 2) * r_dev + inner
        value = keep_ref[q] + got_ref[q].astype(f32)
        if rows + q < got_ref.shape[0]:
            value = value + got_ref[rows + q].astype(f32)
        if owner % 2 == 0:
            next_ref[row] = value
        elif send_ref.dtype == f32:
            send_ref[row] = value
        else:
            high, low = split_two(value)
            send_ref[row] = high
            if rows // 2 + row < send_ref.shape[0]:
                send_ref[rows // 2 + row] = low


def lead_kernel(out_ref):
    out_ref[...] = jnp.zeros_like(out_ref)


def table_kernel(orb_ref, split_ref, _, left_ref, member_ref, mask_ref):
    mag = split_ref.shape[0]
    natom = orb_ref.shape[0]
    row, col = iota((mag, mag), 0), iota((mag, mag), 1)
    same = jnp.zeros((mag, mag), jnp.bool_)
    tall = iota((2 * mag, LANES), 0) % mag
    tall_lane = iota((2 * mag, LANES), 1)
    rows = iota((mag, LANES), 0)
    member = jnp.zeros((2 * mag, LANES), jnp.bool_)
    for i, (start, stop) in enumerate(spans([orb_ref[i] for i in range(natom)])):
        same = same | ((row >= start) & (row < stop) & (col >= start) & (col < stop))
        member = member | ((tall >= start) & (tall < stop) & (tall_lane == i))
        mask_ref[i] = jnp.where((rows >= start) & (rows < stop), -inv_four_pi, 0.0)
    split = split_ref[...]
    high, low = split_two(jnp.where(same, 0.5 * (split + split.T), 0.0))
    left_ref[:, 0:mag] = high
    left_ref[:, mag : 2 * mag] = high
    left_ref[:, 2 * mag :] = low
    member_ref[...] = jnp.where(member, 1.0, 0.0).astype(bf16)


def exchange_kernel(group, keep_ref, got_ref, left_ref, member_ref, mask_ref, out_ref):
    mag = left_ref.shape[0]
    natom = mask_ref.shape[0]
    for row in range(keep_ref.shape[0]):
        value = keep_ref[row] + got_ref[row].astype(f32)
        up, down = [], []
        for c in range(mag // group):
            up.append(value[c * 2 * group : c * 2 * group + group])
            down.append(value[c * 2 * group + group : (c + 1) * 2 * group])
        both = jnp.concatenate(
            [jnp.concatenate(up, axis=0), jnp.concatenate(down, axis=0)], axis=1
        )
        high, low = split_two(both)
        both = jnp.dot(
            left_ref[...],
            jnp.concatenate([high, low, high], axis=0),
            preferred_element_type=f32,
        )
        left = both[:, :LANES]
        right = both[:, LANES:].T
        im_part = left[:, :mag] * right[mag:, :] + left[:, mag:] * right[:mag, :]
        part = jnp.dot(
            jnp.concatenate(split_two(im_part), axis=1),
            member_ref[...],
            preferred_element_type=f32,
        )
        pairs = [jnp.sum(mask_ref[i] * part, axis=0, keepdims=True) for i in range(natom)]
        out_ref[row] = jnp.concatenate(pairs, axis=0)[:, :natom]


def vmem(count):
    return [pl.BlockSpec(memory_space=pltpu.VMEM)] * count


def local(
    axis,
    n,
    eigvecs,
    eigvals,
    kpoints,
    counts,
    energy_real,
    energy_imag,
    offsets,
    atom_orbitals,
    positions,
    exch_split,
):
    nslot, _, norb = eigvals.shape
    mag = eigvecs.shape[2]
    natom = atom_orbitals.shape[0]
    total = offsets.shape[1]
    r_dev = total // n
    srow = -(-nslot // 32) * 32
    group = 256 // srow
    rows = total // 2
    lead = pl.pallas_call(
        lead_kernel,
        out_shape=jax.ShapeDtypeStruct((SUB, LANES), f32),
        out_specs=vmem(1)[0],
        compiler_params=pltpu.CompilerParams(vmem_limit_bytes=1 << 20),
        cost_estimate=pl.CostEstimate(flops=1 << 32, bytes_accessed=1 << 23, transcendentals=0),
        name="lead",
    )()
    keep, send = pl.pallas_call(
        functools.partial(green_kernel, axis, r_dev),
        out_shape=(
            jax.ShapeDtypeStruct((rows, 2 * mag, LANES), f32),
            jax.ShapeDtypeStruct((rows, 2 * mag, LANES), f32),
        ),
        in_specs=[pl.BlockSpec(memory_space=pltpu.SMEM)] * 3
        + vmem(6)
        + [pl.BlockSpec(memory_space=pl.ANY)],
        out_specs=tuple(vmem(2)),
        scratch_shapes=[
            pltpu.VMEM((SUB, LANES), f32),
            pltpu.VMEM((norb // LANES, 2 * srow, LANES), f32),
            pltpu.VMEM((natom, srow, LANES), f32),
            pltpu.VMEM((natom, srow, LANES), f32),
            pltpu.VMEM((2, 2 * mag, 2 * norb), bf16),
            pltpu.VMEM((2, 3, mag, norb), f32),
            pltpu.VMEM((2, srow, norb), f32),
            pltpu.VMEM((2, srow, norb), f32),
            pltpu.VMEM((2, srow, norb), f32),
        ]
        + [pltpu.VMEM((GROUPS * group * srow, 2 * norb), bf16)] * 4,
        compiler_params=pltpu.CompilerParams(vmem_limit_bytes=16 << 20),
        name="green",
    )(
        counts,
        energy_real,
        energy_imag,
        eigvecs,
        eigvals,
        kpoints,
        offsets,
        atom_orbitals,
        positions,
        lead,
    )
    tables = pl.pallas_call(
        table_kernel,
        out_shape=(
            jax.ShapeDtypeStruct((mag, 3 * mag), bf16),
            jax.ShapeDtypeStruct((2 * mag, LANES), bf16),
            jax.ShapeDtypeStruct((natom, mag, LANES), f32),
        ),
        in_specs=[pl.BlockSpec(memory_space=pltpu.SMEM)] + vmem(1) + [pl.BlockSpec(memory_space=pl.ANY)],
        out_specs=tuple(vmem(3)),
        compiler_params=pltpu.CompilerParams(vmem_limit_bytes=4 << 20),
        name="tables",
    )(atom_orbitals, exch_split, keep)
    bit = 1
    while True:
        got = lax.ppermute(send, axis, [(d, d ^ crossed(bit, d, n)) for d in range(n)])
        bit *= 2
        if bit == n:
            break
        rows //= 2
        sent = jax.ShapeDtypeStruct((rows, 2 * mag, LANES), f32)
        if bit == 2 and rows >= 2:
            sent = jax.ShapeDtypeStruct((rows + rows // 2, 2 * mag, LANES), bf16)
        keep, send = pl.pallas_call(
            functools.partial(add_kernel, r_dev),
            out_shape=(
                jax.ShapeDtypeStruct((rows, 2 * mag, LANES), f32),
                sent,
            ),
            in_specs=vmem(2),
            out_specs=tuple(vmem(2)),
            compiler_params=pltpu.CompilerParams(vmem_limit_bytes=4 << 20),
            name="add",
        )(keep, got)
    return pl.pallas_call(
        functools.partial(exchange_kernel, group),
        out_shape=jax.ShapeDtypeStruct((r_dev, natom, natom), f32),
        in_specs=vmem(5),
        out_specs=vmem(1)[0],
        compiler_params=pltpu.CompilerParams(vmem_limit_bytes=4 << 20),
        name="exchange",
    )(keep, got, *tables)


def solution(mesh):
    placed = (
        P("ka", None, None, None),
        P("ka", None, None),
        P(None, "ka"),
        P("ka"),
        P("grp"),
        P("grp"),
        P(),
        P(),
        P(),
        P(),
    )
    return jax.shard_map(
        functools.partial(local, "ka", mesh.shape["ka"]),
        mesh=mesh,
        in_specs=placed,
        out_specs=P(("grp", "ka"), None, None),
        check_vma=False,
    )
```

```python
import functools

import jax
import jax.numpy as jnp
from jax import lax
from jax.experimental import pallas as pl
from jax.experimental.pallas import tpu as pltpu
from jax.sharding import PartitionSpec as P


inv_four_pi = 0.25 / 3.141592653589793
two_pi = 2.0 * 3.141592653589793
f32 = jnp.float32
bf16 = jnp.bfloat16
LANES = 128
SUB = 8
GROUPS = 4


def iota(shape, dim):
    return lax.broadcasted_iota(jnp.int32, shape, dim)


def crossed(position, device, n):
    if n < 16:
        return position
    differ = ((position >> 1) ^ (position >> 2)) & device & 1
    return position ^ (differ * 6)


def spans(sizes):
    start, found = jnp.int32(0), []
    for size in sizes:
        stop = start + size
        found.append((start, stop))
        start = stop
    return found


def split_two(x):
    high = x.astype(bf16)
    return high, (x - high.astype(f32)).astype(bf16)


def green_kernel(
    axis,
    r_dev,
    cnt_ref,
    er_ref,
    ei_ref,
    vec_ref,
    lev_ref,
    k_ref,
    off_ref,
    orb_ref,
    pos_ref,
    _,
    keep_ref,
    send_ref,
    kpad_ref,
    wide_ref,
    cos_ref,
    sin_ref,
    right_ref,
    sum_ref,
    f1_ref,
    f2_ref,
    f3_ref,
    *scaled_refs,
):
    nslot = lev_ref.shape[0]
    mag, norb = vec_ref.shape[2], vec_ref.shape[3] // 2
    natom = orb_ref.shape[0]
    srow = f1_ref.shape[1]
    total = off_ref.shape[1]
    half = total // 2
    group = 256 // srow
    me = lax.axis_index(axis)
    kpad_ref[...] = jnp.zeros_like(kpad_ref)
    wide_ref[:, 2 * nslot :, :] = jnp.zeros_like(wide_ref[:, 2 * nslot :, :])

    kpad_ref[0:3, 0:nslot] = k_ref[...].astype(f32)
    kwide = kpad_ref[...]
    ktall = kwide.T
    klane = kwide
    for step in range(1, LANES // srow):
        klane = klane + pltpu.roll(kwide, step * srow, 1)

    orb_row = orb_ref[...].astype(f32).reshape(1, natom)
    sizes = [
        jnp.sum(jnp.where(iota((1, natom), 1) == i, orb_row, 0.0)).astype(jnp.int32)
        for i in range(natom)
    ]
    bounds = spans(sizes)
    lane = iota((1, LANES), 1)
    orbital = jnp.where(lane >= mag, lane - mag, lane)
    kpos = jnp.zeros((srow, LANES), f32)
    kat = jnp.zeros((srow, LANES), f32)
    for x in range(3):
        site = jnp.zeros((1, LANES), f32)
        atom = jnp.zeros((1, LANES), f32)
        for i, (start, stop) in enumerate(bounds):
            where = pos_ref[x : x + 1, i : i + 1]
            site = jnp.where((orbital >= start) & (orbital < stop), where, site)
            atom = jnp.where(lane == i, where, atom)
        kpos = kpos + ktall[0:srow, x : x + 1] * site
        kat = kat + ktall[0:srow, x : x + 1] * atom
    cos_pos, sin_pos = jnp.cos(two_pi * kpos), jnp.sin(two_pi * kpos)
    cos_atom, sin_atom = jnp.cos(two_pi * kat), jnp.sin(two_pi * kat)
    first = iota((srow, LANES), 1) < mag
    cos_sgn = jnp.where(first, -cos_pos, cos_pos)
    sin_sgn = jnp.where(first, -sin_pos, sin_pos)
    for i in range(natom):
        cos_a, sin_a = cos_atom[:, i : i + 1], sin_atom[:, i : i + 1]
        cos_ref[i] = cos_pos * cos_a + sin_pos * sin_a
        sin_ref[i] = sin_sgn * cos_a - cos_sgn * sin_a

    lane = iota((1, LANES), 1) % srow
    count = cnt_ref[0]
    inverse = jnp.full((1, LANES), count, jnp.int32).astype(f32)
    inverse = (1.0 / inverse).astype(bf16).astype(f32)
    weight = jnp.where(lane < count, inverse, 0.0)
    repeat = group * srow // LANES
    own = (iota((SUB, group * srow), 1) // srow) == iota((SUB, group * srow), 0)
    blocks = []
    for base in range(0, half, SUB):
        place = iota((SUB, total), 0) + base
        owner = place // r_dev if r_dev > 1 else place
        odd = owner & 1
        owner = crossed(owner - odd, me ^ odd, total // r_dev) ^ me ^ odd
        wanted = owner * r_dev + place % r_dev if r_dev > 1 else owner
        pick = iota((SUB, total), 1) == wanted
        angle = jnp.zeros((SUB, LANES), f32)
        for x in range(3):
            off = jnp.where(pick, off_ref[x : x + 1, :].astype(f32), 0.0)
            angle = angle + jnp.sum(off, axis=1, keepdims=True) * klane[x : x + 1, :]
        angle = two_pi * angle
        rows = []
        for wave in (jnp.cos(angle) * weight, jnp.sin(angle) * weight):
            wave = jnp.concatenate([wave] * repeat, axis=1)
            for r in range(SUB):
                rows.append(jnp.where(own, wave[r : r + 1, :], 0.0))
        blocks.append(jnp.concatenate(rows, axis=0).astype(bf16))
    flip = jnp.where(iota((SUB, LANES), 1) < mag, 1.0, -1.0).astype(f32)

    er, ei = er_ref[0], ei_ref[0]
    for s in range(nslot):
        wide = lev_ref[s].astype(f32)
        for t in range(norb // LANES):
            wide_ref[t, 2 * s : 2 * s + 2, :] = wide[:, t * LANES : (t + 1) * LANES]
    for spin in range(2):
        for t in range(norb // LANES):
            lanes = slice(t * LANES, (t + 1) * LANES)
            shift = er - wide_ref.at[t][pl.ds(spin, srow, stride=2), :]
            inv = 1.0 / (shift * shift + ei * ei)
            fr = shift * inv
            fi = -(ei * inv)
            f1_ref[spin, :, lanes] = fr
            f2_ref[spin, :, lanes] = fi - fr
            f3_ref[spin, :, lanes] = fi + fr
    for spin in range(2):
        re_vec = vec_ref[0, spin, :, :norb]
        im_vec = vec_ref[0, spin, :, norb:]
        right_ref[spin, :mag, :norb] = re_vec
        right_ref[spin, :mag, norb:] = im_vec
        right_ref[spin, mag:, :norb] = -im_vec
        right_ref[spin, mag:, norb:] = re_vec
        re_wide = re_vec.astype(f32)
        im_wide = im_vec.astype(f32)
        sum_ref[spin, 0] = re_wide + im_wide
        sum_ref[spin, 1] = re_wide
        sum_ref[spin, 2] = im_wide

    def product(chunk, spin):
        buf = scaled_refs[(chunk % 2) * 2 + spin]
        for j in range(group * GROUPS):
            a = chunk * group * GROUPS + j
            both = f1_ref[spin] * sum_ref[spin, 0, a : a + 1, :]
            cross = f2_ref[spin] * sum_ref[spin, 1, a : a + 1, :]
            other = f3_ref[spin] * sum_ref[spin, 2, a : a + 1, :]
            buf[j * srow : (j + 1) * srow, :norb] = (both - other).astype(bf16)
            buf[j * srow : (j + 1) * srow, norb:] = (both + cross).astype(bf16)
        return lax.dot_general(
            buf[...], right_ref[spin], (((1,), (1,)), ((), ())), preferred_element_type=f32
        )

    def fourier(chunk, green):
        for sub in range(GROUPS):
            c = chunk * GROUPS + sub
            turned = [[], []]
            for j in range(group):
                a = c * group + j
                atom = jnp.int32(0)
                for _, stop in bounds[:-1]:
                    atom = atom + (a >= stop).astype(jnp.int32)
                cos_phase, sin_phase = cos_ref[atom], sin_ref[atom]
                for spin in range(2):
                    at = (sub * group + j) * srow
                    g = green[spin][at : at + srow, :]
                    turned[spin].append(g * cos_phase + pltpu.roll(g, mag, 1) * sin_phase)
            stack = jnp.concatenate(
                [jnp.concatenate(turned[spin], axis=0).astype(bf16) for spin in range(2)], axis=1
            )
            for b, block in enumerate(blocks):
                res = jnp.dot(block, stack, preferred_element_type=f32)
                for r in range(SUB):
                    plus, minus = [], []
                    for spin in range(2):
                        lanes = slice(spin * LANES, (spin + 1) * LANES)
                        even = res[r * SUB : (r + 1) * SUB, lanes]
                        odd = res[(SUB + r) * SUB : (SUB + r + 1) * SUB, lanes]
                        odd = pltpu.roll(odd, mag, 1) * flip
                        plus.append(even + odd if spin == 0 else even - odd)
                        minus.append(even - odd if spin == 0 else even + odd)
                    for p, pieces in ((b * SUB + r, plus), (b * SUB + r + half, minus)):
                        owner, inner = p // r_dev, p % r_dev
                        row = (owner // 2) * r_dev + inner
                        block_out = jnp.concatenate(pieces, axis=0)
                        rows = slice(c * 2 * group, (c + 1) * 2 * group)
                        if owner % 2 == 0:
                            keep_ref[row, rows, :] = block_out
                        else:
                            send_ref[row, rows, :] = block_out.astype(send_ref.dtype)

    last = None
    for chunk in range(mag // (group * GROUPS)):
        green = [product(chunk, 0), product(chunk, 1)]
        if last is not None:
            fourier(chunk - 1, last)
        last = green
    fourier(mag // (group * GROUPS) - 1, last)


def add_kernel(r_dev, keep_ref, got_ref, next_ref, send_ref):
    rows = keep_ref.shape[0]
    for q in range(rows):
        owner, inner = q // r_dev, q % r_dev
        row = (owner // 2) * r_dev + inner
        value = keep_ref[q] + got_ref[q].astype(f32)
        if rows + q < got_ref.shape[0]:
            value = value + got_ref[rows + q].astype(f32)
        if owner % 2 == 0:
            next_ref[row] = value
        elif send_ref.dtype == f32:
            send_ref[row] = value
        else:
            high, low = split_two(value)
            send_ref[row] = high
            if rows // 2 + row < send_ref.shape[0]:
                send_ref[rows // 2 + row] = low


def lead_kernel(out_ref):
    out_ref[...] = jnp.zeros_like(out_ref)


def table_kernel(orb_ref, split_ref, _, left_ref, member_ref, mask_ref):
    mag = split_ref.shape[0]
    natom = orb_ref.shape[0]
    row, col = iota((mag, mag), 0), iota((mag, mag), 1)
    same = jnp.zeros((mag, mag), jnp.bool_)
    tall = iota((2 * mag, LANES), 0) % mag
    tall_lane = iota((2 * mag, LANES), 1)
    rows = iota((mag, LANES), 0)
    member = jnp.zeros((2 * mag, LANES), jnp.bool_)
    for i, (start, stop) in enumerate(spans([orb_ref[i] for i in range(natom)])):
        same = same | ((row >= start) & (row < stop) & (col >= start) & (col < stop))
        member = member | ((tall >= start) & (tall < stop) & (tall_lane == i))
        mask_ref[i] = jnp.where((rows >= start) & (rows < stop), -inv_four_pi, 0.0)
    split = split_ref[...]
    high, low = split_two(jnp.where(same, 0.5 * (split + split.T), 0.0))
    left_ref[:, 0:mag] = high
    left_ref[:, mag : 2 * mag] = high
    left_ref[:, 2 * mag :] = low
    member_ref[...] = jnp.where(member, 1.0, 0.0).astype(bf16)


def exchange_kernel(group, keep_ref, got_ref, left_ref, member_ref, mask_ref, out_ref):
    mag = left_ref.shape[0]
    natom = mask_ref.shape[0]
    for row in range(keep_ref.shape[0]):
        value = keep_ref[row] + got_ref[row].astype(f32)
        up, down = [], []
        for c in range(mag // group):
            up.append(value[c * 2 * group : c * 2 * group + group])
            down.append(value[c * 2 * group + group : (c + 1) * 2 * group])
        both = jnp.concatenate(
            [jnp.concatenate(up, axis=0), jnp.concatenate(down, axis=0)], axis=1
        )
        high, low = split_two(both)
        both = jnp.dot(
            left_ref[...],
            jnp.concatenate([high, low, high], axis=0),
            preferred_element_type=f32,
        )
        left = both[:, :LANES]
        right = both[:, LANES:].T
        im_part = left[:, :mag] * right[mag:, :] + left[:, mag:] * right[:mag, :]
        part = jnp.dot(
            jnp.concatenate(split_two(im_part), axis=1),
            member_ref[...],
            preferred_element_type=f32,
        )
        pairs = [jnp.sum(mask_ref[i] * part, axis=0, keepdims=True) for i in range(natom)]
        out_ref[row] = jnp.concatenate(pairs, axis=0)[:, :natom]


def vmem(count):
    return [pl.BlockSpec(memory_space=pltpu.VMEM)] * count


def local(
    axis,
    n,
    eigvecs,
    eigvals,
    kpoints,
    counts,
    energy_real,
    energy_imag,
    offsets,
    atom_orbitals,
    positions,
    exch_split,
):
    nslot, _, norb = eigvals.shape
    mag = eigvecs.shape[2]
    natom = atom_orbitals.shape[0]
    total = offsets.shape[1]
    r_dev = total // n
    srow = -(-nslot // 32) * 32
    group = 256 // srow
    rows = total // 2
    lead = pl.pallas_call(
        lead_kernel,
        out_shape=jax.ShapeDtypeStruct((SUB, LANES), f32),
        out_specs=vmem(1)[0],
        compiler_params=pltpu.CompilerParams(vmem_limit_bytes=1 << 20),
        cost_estimate=pl.CostEstimate(flops=1 << 32, bytes_accessed=1 << 23, transcendentals=0),
        name="lead",
    )()
    keep, send = pl.pallas_call(
        functools.partial(green_kernel, axis, r_dev),
        out_shape=(
            jax.ShapeDtypeStruct((rows, 2 * mag, LANES), f32),
            jax.ShapeDtypeStruct((rows, 2 * mag, LANES), f32),
        ),
        in_specs=[pl.BlockSpec(memory_space=pltpu.SMEM)] * 3
        + vmem(6)
        + [pl.BlockSpec(memory_space=pl.ANY)],
        out_specs=tuple(vmem(2)),
        scratch_shapes=[
            pltpu.VMEM((SUB, LANES), f32),
            pltpu.VMEM((norb // LANES, 2 * srow, LANES), f32),
            pltpu.VMEM((natom, srow, LANES), f32),
            pltpu.VMEM((natom, srow, LANES), f32),
            pltpu.VMEM((2, 2 * mag, 2 * norb), bf16),
            pltpu.VMEM((2, 3, mag, norb), f32),
            pltpu.VMEM((2, srow, norb), f32),
            pltpu.VMEM((2, srow, norb), f32),
            pltpu.VMEM((2, srow, norb), f32),
        ]
        + [pltpu.VMEM((GROUPS * group * srow, 2 * norb), bf16)] * 4,
        compiler_params=pltpu.CompilerParams(vmem_limit_bytes=16 << 20),
        name="green",
    )(
        counts,
        energy_real,
        energy_imag,
        eigvecs,
        eigvals,
        kpoints,
        offsets,
        atom_orbitals,
        positions,
        lead,
    )
    tables = pl.pallas_call(
        table_kernel,
        out_shape=(
            jax.ShapeDtypeStruct((mag, 3 * mag), bf16),
            jax.ShapeDtypeStruct((2 * mag, LANES), bf16),
            jax.ShapeDtypeStruct((natom, mag, LANES), f32),
        ),
        in_specs=[pl.BlockSpec(memory_space=pltpu.SMEM)] + vmem(1) + [pl.BlockSpec(memory_space=pl.ANY)],
        out_specs=tuple(vmem(3)),
        compiler_params=pltpu.CompilerParams(vmem_limit_bytes=4 << 20),
        name="tables",
    )(atom_orbitals, exch_split, keep)
    bit = 1
    while True:
        got = lax.ppermute(send, axis, [(d, d ^ crossed(bit, d, n)) for d in range(n)])
        bit *= 2
        if bit == n:
            break
        rows //= 2
        sent = jax.ShapeDtypeStruct((rows, 2 * mag, LANES), f32)
        if bit == 2 and rows >= 2:
            sent = jax.ShapeDtypeStruct((rows + 3 * rows // 4, 2 * mag, LANES), bf16)
        keep, send = pl.pallas_call(
            functools.partial(add_kernel, r_dev),
            out_shape=(
                jax.ShapeDtypeStruct((rows, 2 * mag, LANES), f32),
                sent,
            ),
            in_specs=vmem(2),
            out_specs=tuple(vmem(2)),
            compiler_params=pltpu.CompilerParams(vmem_limit_bytes=4 << 20),
            name="add",
        )(keep, got)
    return pl.pallas_call(
        functools.partial(exchange_kernel, group),
        out_shape=jax.ShapeDtypeStruct((r_dev, natom, natom), f32),
        in_specs=vmem(5),
        out_specs=vmem(1)[0],
        compiler_params=pltpu.CompilerParams(vmem_limit_bytes=4 << 20),
        name="exchange",
    )(keep, got, *tables)


def solution(mesh):
    placed = (
        P("ka", None, None, None),
        P("ka", None, None),
        P(None, "ka"),
        P("ka"),
        P("grp"),
        P("grp"),
        P(),
        P(),
        P(),
        P(),
    )
    return jax.shard_map(
        functools.partial(local, "ka", mesh.shape["ka"]),
        mesh=mesh,
        in_specs=placed,
        out_specs=P(("grp", "ka"), None, None),
        check_vma=False,
    )
```
